32 devices in a mesh: groups: 2 (over y), frame: 8 (over z, x), head: 2 (over core).
Axes of the slice: x: 2, y: 2, z: 4, core: 2. Of those that a mesh axis runs over, the one named last changes fastest.
Arguments:
- stream: bfloat16 [2048, 2240], P(('groups', 'frame'), 'head'), parts along dimension 0, may hold values from -24 to 24
- queries: bfloat16 [2048, 1120], P(('groups', 'frame'), 'head'), parts along dimension 0, may hold values from -6 to 6
- key_rows: bfloat16 [2048, 1120], P(('groups', 'frame'), 'head'), parts along dimension 0, may hold values from -6 to 6
- value_rows: bfloat16 [2048, 1120], P(('groups', 'frame'), 'head'), parts along dimension 0, may hold values from -16 to 16
- attn_gain: float32 [1120], P('head'), may hold values from 0.25 to 1.75
- w_out: bfloat16 [1120, 2240], P('head', 'frame'), may hold values from -0.1875 to 0.1875
- ffn_gain: float32 [2240], replicated, may hold values from 0.25 to 1.75
- w_up: bfloat16 [2240, 3360], P('frame', 'head'), may hold values from -0.125 to 0.125
- conv_taps: float32 [3, 3360], P(None, 'head'), may hold values from -3 to 3
- w_down: bfloat16 [3360, 2240], P('head', 'frame'), may hold values from -0.109375 to 0.109375
Outputs:
- block_out: bfloat16 [2048, 2240], P(('groups', 'frame'), 'head'), parts along dimension 0
The draws below stay inside these ranges and needn't reach their ends.
There are 2 independent parts, one for each index of `groups`. The reference program is written for one: setup_inputs(seed, part) draws one part's arguments, and reference() takes and returns one part's arrays. A program takes and returns all parts, laid end to end along the dimension named above; an argument that names none is the same for every part. Nothing has to cross between parts.
All inputs are finite; a program needn't handle non-finite values.
Results may differ from the reference program's by a relative error of at most 0.0058.
Values may be sent and summed in bfloat16 or wider, within the bound.
A program may use at most 128 MiB of HBM per device.

```python
import math
import jax
import jax.numpy as jnp
from jax import lax

D = 2240
HEADS = 10
HEAD_DIM = 112
FF = 3360
TPF = 128
FRAMES = 8
TOKENS = 1024


def draw_stream(key, part):
    subkeys = jax.random.split(key, 3)
    columns = jnp.arange(D, dtype=jnp.float32) / (D - 1)
    col_scale = 3.0 ** columns * jax.random.uniform(subkeys[0], (D,), jnp.float32, 0.7, 1.4)
    row_scale = jnp.exp(jax.random.uniform(subkeys[1], (TOKENS, 1), jnp.float32, math.log(0.5), math.log(2.0)))
    base = jnp.clip(jax.random.normal(subkeys[2], (TOKENS, D), jnp.float32), -6.0, 6.0)
    values = jnp.clip(0.5 * base * row_scale * col_scale, -24.0, 24.0)
    return values.astype(jnp.bfloat16)


def draw_value_rows(key, part):
    subkeys = jax.random.split(key, 2)
    width = HEADS * HEAD_DIM
    head_of = (jnp.arange(width) // HEAD_DIM).astype(jnp.float32)
    head_scale = 10.0 ** (head_of / max(HEADS - 1, 1))
    channel = jax.random.uniform(subkeys[0], (width,), jnp.float32, 0.7, 1.4)
    base = jnp.clip(jax.random.normal(subkeys[1], (TOKENS, width), jnp.float32), -4.0, 4.0)
    values = jnp.clip(0.3 * base * head_scale * channel, -16.0, 16.0)
    return values.astype(jnp.bfloat16)


def shard_levels(own_key, dims, cuts, low, top_value):
    loudness, own = 1.0, jax.random.fold_in(own_key, 6)
    for axis_at, parts in cuts:
        steps = jnp.exp(jax.random.uniform(jax.random.fold_in(own, axis_at), (parts,), jnp.float32, low / len(cuts), top_value / len(cuts)))
        loudness = loudness * jnp.repeat(steps, dims[axis_at] // parts).reshape([-1 if axis == axis_at else 1 for axis in range(len(dims))])
    return loudness


def noise(rng, shape, scale, limit, cuts=(), kind=jnp.bfloat16):
    array = jax.random.normal(rng, shape, jnp.float32) * scale
    if len(cuts) > 0:
        array = shard_levels(rng, shape, cuts, -0.22, 0.18) * array
    return jnp.clip(array, min=-limit, max=limit).astype(kind)


def setup_inputs(seed: int = 0, part: int = 0) -> dict:
    arg_keys = jax.random.split(jax.random.key(seed), 11)
    own_keys = jax.random.split(jax.random.fold_in(arg_keys[10], part), 11)
    stream = draw_stream(jax.random.fold_in(jax.random.fold_in(arg_keys[10], part), 71), part)
    queries = noise(own_keys[1], (TOKENS, HEADS * HEAD_DIM), 1.0, 6.0, ((0, 8), (1, 2)))
    key_rows = noise(own_keys[2], (TOKENS, HEADS * HEAD_DIM), 1.0, 6.0, ((0, 8), (1, 2)))
    value_rows = draw_value_rows(jax.random.fold_in(jax.random.fold_in(arg_keys[10], part), 71), part)
    attn_gain = jnp.clip(1.0 + 0.15 * jax.random.normal(arg_keys[4], (HEADS * HEAD_DIM,), jnp.float32), 0.25, 1.75)
    w_out = noise(arg_keys[5], (HEADS * HEAD_DIM, D), (HEADS * HEAD_DIM) ** -0.5, 0.1875, ((0, 2), (1, 8)))
    ffn_gain = jnp.clip(1.0 + 0.15 * jax.random.normal(arg_keys[6], (D,), jnp.float32), 0.25, 1.75)
    w_up = noise(arg_keys[7], (D, FF), D ** -0.5, 0.125, ((0, 8), (1, 2)))
    conv_taps = noise(arg_keys[8], (3, FF), 0.7, 3.0, ((1, 2),), jnp.float32)
    w_down = noise(arg_keys[9], (FF, D), FF ** -0.5, 0.109375, ((0, 2), (1, 8)))
    return dict(stream=stream, queries=queries, key_rows=key_rows, value_rows=value_rows, attn_gain=attn_gain, w_out=w_out, ffn_gain=ffn_gain, w_up=w_up, conv_taps=conv_taps, w_down=w_down)


def reference(stream, queries, key_rows, value_rows, attn_gain, w_out, ffn_gain, w_up, conv_taps, w_down):
    highest = lax.Precision.HIGHEST
    qpos = jnp.maximum(queries.astype(jnp.float32), 0.0).reshape(FRAMES, TPF, HEADS, HEAD_DIM)
    kpos = jnp.maximum(key_rows.astype(jnp.float32), 0.0).reshape(FRAMES, TPF, HEADS, HEAD_DIM)
    values = value_rows.astype(jnp.float32).reshape(FRAMES, TPF, HEADS, HEAD_DIM)
    frame_state = jnp.einsum('fthb,fthc->fhbc', kpos, values, precision=highest)
    frame_keys = lax.optimization_barrier(jnp.sum(kpos, axis=1))
    state = jnp.cumsum(frame_state, axis=0)
    key_total = jnp.cumsum(frame_keys, axis=0)
    numer = jnp.einsum('fthb,fhbc->fthc', qpos, state, precision=highest)
    denom = jnp.einsum('fthb,fhb->fth', qpos, key_total, precision=highest) + 1e-06
    attended = (numer / denom[..., None]).reshape(TOKENS, HEADS * HEAD_DIM)
    scale = lax.rsqrt(lax.optimization_barrier(jnp.mean(attended * attended, axis=1, keepdims=True)) + 1e-06)
    normed = (attended * scale * attn_gain).astype(jnp.bfloat16)
    proj = jnp.dot(normed, w_out, preferred_element_type=jnp.float32)
    resid = (stream.astype(jnp.float32) + proj).astype(jnp.bfloat16)
    resid = lax.optimization_barrier(resid)
    resid_float = resid.astype(jnp.float32)
    inverse = lax.rsqrt(lax.optimization_barrier(jnp.mean(resid_float * resid_float, axis=1, keepdims=True)) + 1e-06)
    ffn_in = (resid_float * inverse * ffn_gain).astype(jnp.bfloat16)
    hidden = jax.nn.silu(jnp.dot(ffn_in, w_up, preferred_element_type=jnp.float32)).astype(jnp.bfloat16)
    hidden = lax.optimization_barrier(hidden)
    framed = hidden.astype(jnp.float32).reshape(FRAMES, TPF, FF)
    padded = jnp.pad(framed, ((1, 1), (0, 0), (0, 0)))
    mixed = conv_taps[0] * padded[:-2] + conv_taps[1] * padded[1:-1] + conv_taps[2] * padded[2:]
    mixed = mixed.astype(jnp.bfloat16).reshape(TOKENS, FF)
    ffn_out = jnp.dot(mixed, w_down, preferred_element_type=jnp.float32)
    return (resid_float + ffn_out).astype(jnp.bfloat16)
```

```python
import functools

import jax
import jax.numpy as jnp
from jax import lax
from jax.experimental import pallas as pl
from jax.experimental.pallas import tpu as pltpu
from jax.sharding import PartitionSpec as P

D = 2240
HEADS = 10
HEAD_DIM = 112
TPF = 128


def prefix(x, axis, combine, identity):
    length, place = (lax.axis_size(axis), lax.axis_index(axis))
    everything = jax.tree.map(lambda part: lax.all_gather(part, axis), x)
    start = jax.tree.map(
        lambda part, zero: jnp.broadcast_to(jnp.asarray(zero, part.dtype), part.shape), x, identity
    )

    def hop(k, before):
        reached = k < place
        new = combine(before, jax.tree.map(lambda part: part[k], everything))
        return jax.tree.map(lambda a, b: jnp.where(reached, a, b), new, before)

    return lax.fori_loop(0, length, hop, start)


def padded_2(block, sides, width):
    for axis, dim in sides:
        count = lax.axis_size(axis)
        forward = [(i, i + 1) for i in range(count - 1)]
        backward = [(target, source) for source, target in forward]
        low = lax.ppermute(
            lax.slice_in_dim(block, block.shape[dim] - width, None, axis=dim), axis, forward
        )
        high = lax.ppermute(lax.slice_in_dim(block, 0, width, axis=dim), axis, backward)
        block = jnp.concatenate([low, block, high], axis=dim)
    return block


def add_pair(earlier, later):
    return (earlier[0] + later[0], earlier[1] + later[1])


def body(
    stream, queries, key_rows, value_rows, attn_gain, w_out, ffn_gain, w_up, conv_taps, w_down
):
    highest = lax.Precision.HIGHEST
    tokens_here = queries.shape[0]
    frames_here = tokens_here // TPF
    heads_here = queries.shape[1] // HEAD_DIM
    qpos = jnp.maximum(queries.astype(jnp.float32), 0.0).reshape(
        frames_here, TPF, heads_here, HEAD_DIM
    )
    kpos = jnp.maximum(key_rows.astype(jnp.float32), 0.0).reshape(
        frames_here, TPF, heads_here, HEAD_DIM
    )
    values = value_rows.astype(jnp.float32).reshape(frames_here, TPF, heads_here, HEAD_DIM)
    frame_state = jnp.einsum("fthb,fthc->fhbc", kpos, values, precision=highest)
    frame_keys = jnp.sum(kpos, axis=1)
    own_state = jnp.sum(frame_state, axis=0)
    own_keys = jnp.sum(frame_keys, axis=0)
    empty_state = jnp.zeros_like(own_state)
    empty_keys = jnp.zeros_like(own_keys)
    before_state, before_keys = prefix(
        (own_state, own_keys), "frame", add_pair, (empty_state, empty_keys)
    )
    state = before_state[None] + jnp.cumsum(frame_state, axis=0)
    key_total = before_keys[None] + jnp.cumsum(frame_keys, axis=0)
    numer = jnp.einsum("fthb,fhbc->fthc", qpos, state, precision=highest)
    denom = jnp.einsum("fthb,fhb->fth", qpos, key_total, precision=highest) + 1e-06
    attended = (numer / denom[..., None]).reshape(tokens_here, heads_here * HEAD_DIM)
    squares = lax.psum(jnp.sum(attended * attended, axis=1), "head")
    scale = lax.rsqrt(squares / (HEADS * HEAD_DIM) + 1e-06)
    normed = (attended * scale[:, None] * attn_gain).astype(jnp.bfloat16)
    width_here = stream.shape[1]
    first_col = lax.axis_index("head") * width_here
    gain_here = lax.dynamic_slice_in_dim(ffn_gain, first_col, width_here, 0)
    proj = jnp.dot(
        normed,
        lax.all_gather(w_out, "frame", axis=1, tiled=True),
        preferred_element_type=jnp.float32,
    )
    proj_mine = lax.psum_scatter(proj, "head", scatter_dimension=1, tiled=True)
    resid_mine = (stream.astype(jnp.float32) + proj_mine).astype(jnp.bfloat16)
    resid_mine = lax.optimization_barrier(resid_mine)
    resid_float = resid_mine.astype(jnp.float32)
    total_sq = lax.psum(jnp.sum(resid_float * resid_float, axis=1), "head")
    inverse = lax.rsqrt(total_sq / D + 1e-06)
    normed_part = (resid_float * inverse[:, None] * gain_here).astype(jnp.bfloat16)
    ffn_in = lax.all_gather(normed_part, "head", axis=1, tiled=True)
    hidden_here = w_up.shape[1]
    up_value = jnp.dot(
        ffn_in,
        lax.all_gather(w_up, "frame", axis=0, tiled=True),
        preferred_element_type=jnp.float32,
    )
    hidden = (
        jax.nn.silu(up_value).astype(jnp.bfloat16).reshape(ffn_in.shape[0] // TPF, TPF, hidden_here)
    )
    padded = padded_2(hidden, (("frame", 0),), 1)
    padded_float = padded.astype(jnp.float32)
    mixed = (
        conv_taps[0] * padded_float[:-2]
        + conv_taps[1] * padded_float[1:-1]
        + conv_taps[2] * padded_float[2:]
    )
    mixed = mixed.astype(jnp.bfloat16).reshape(tokens_here, hidden_here)
    ffn_terms = jnp.dot(
        mixed,
        lax.all_gather(w_down, "frame", axis=1, tiled=True),
        preferred_element_type=jnp.float32,
    )
    ffn_mine = lax.psum_scatter(ffn_terms, "head", scatter_dimension=1, tiled=True)
    return (resid_float + ffn_mine).astype(jnp.bfloat16)


MESH_ID = pl.DeviceIdType.MESH


def ring_frame(pos, n):
    late = pos // (n // 2)
    return (1 - late) * (2 * pos) + late * (2 * (n - 1 - pos) + 1)


def ring_place(frame, n):
    odd = frame % 2
    return (1 - odd) * (frame // 2) + odd * (n - 1 - frame // 2)


def greet(partners):
    barrier = pltpu.get_barrier_semaphore()
    for partner in partners:
        pl.semaphore_signal(barrier, inc=1, device_id=partner, device_id_type=MESH_ID)
    pl.semaphore_wait(barrier, len(partners))


def remote(src, dst, send, recv, device):
    return pltpu.make_async_remote_copy(
        src_ref=src, dst_ref=dst, send_sem=send, recv_sem=recv,
        device_id=device, device_id_type=MESH_ID,
    )


def ring_steps(n):
    far = n // 2
    return [
        (step, way, half)
        for step in range(1, far + 1)
        for half in range(2)
        for way in range(2)
        if step < far or way == half
    ]


def ring_gather(buffer, place, n, send, recv, on_arrival):
    ends = [ring_frame((place + 1) % n, n), ring_frame((place + n - 1) % n, n)]
    started = []

    def origin(step, way):
        back = step if way == 0 else n - step
        return ring_frame((place + n - back) % n, n)

    def arrive(step, way, half):
        source = origin(step, way)
        slot = buffer(source, half)
        remote(slot, slot, send.at[way, step, half], recv.at[way, step, half],
               {"frame": ends[way]}).wait_recv()
        on_arrival(source, half)

    for step, way, half in ring_steps(n):
        if step > 1:
            arrive(step - 1, way, half)
        slot = buffer(origin(step - 1, way), half)
        copy = remote(slot, slot, send.at[way, step, half], recv.at[way, step, half],
                      {"frame": ends[way]})
        copy.start()
        started.append(copy)
    for step, way, half in ring_steps(n):
        last = n // 2 if way == half else n // 2 - 1
        if step == last:
            arrive(step, way, half)
    for copy in started:
        copy.wait_send()


def first_kernel(n, state_ref, up_ref, down_ref, states, up_out, down_out, here,
                 ring_send, ring_recv, all_send, all_recv):
    frame = lax.axis_index("frame")
    place = ring_place(frame, n)
    local = [
        pltpu.make_async_copy(state_ref, states.at[frame], here.at[0]),
        pltpu.make_async_copy(up_ref.at[frame], up_out.at[frame], here.at[1]),
        pltpu.make_async_copy(down_ref.at[frame], down_out.at[frame], here.at[2]),
    ]
    for copy in local:
        copy.start()
    greet([{"frame": (frame + k) % n} for k in range(1, n)])
    local[0].wait()
    pushes = []
    for at, (src, dst) in enumerate(((up_ref, up_out), (down_ref, down_out))):
        for k in range(1, n):
            target = (frame + k) % n
            copy = remote(src.at[target], dst.at[frame], all_send.at[at, k],
                          all_recv.at[at, k], {"frame": target})
            pushes.append((copy, at, k))
    for copy, at, k in pushes:
        copy.start()
    ring_gather(lambda source, half: states.at[source, half], place, n,
                ring_send, ring_recv, lambda source, half: None)
    for copy, at, k in pushes:
        copy.wait_send()
        source = (frame + n - k) % n
        dst = (up_out, down_out)[at]
        remote(dst.at[source], dst.at[source], all_send.at[at, k], all_recv.at[at, k],
               {"frame": source}).wait_recv()
    local[1].wait()
    local[2].wait()


def second_kernel(n, features, width, own_ref, other_ref, sq_ref, stream_ref, gain_ref,
                  everything, resid, arrived, sq_in, sq_mine, sq_two,
                  pair_send, pair_recv, ring_send, ring_recv, twin_send, twin_recv):
    frame, head = lax.axis_index("frame"), lax.axis_index("head")
    place = ring_place(frame, n)
    twin = {"head": 1 - head}
    greet([twin, {"frame": ring_frame((place + 1) % n, n)},
           {"frame": ring_frame((place + n - 1) % n, n)}])
    first = remote(other_ref, arrived, pair_send.at[0], pair_recv.at[0], twin)
    second = remote(sq_ref, sq_in, pair_send.at[1], pair_recv.at[1], twin)
    second.start()
    first.start()
    second.wait()
    scale = lax.rsqrt((sq_ref[...] + sq_in[...])[:, :1] / features + 1e-06)
    first.wait()
    value = stream_ref[...].astype(jnp.float32) + (own_ref[...] + arrived[...]) * scale
    rounded = value.astype(jnp.bfloat16)
    resid[...] = rounded
    value = rounded.astype(jnp.float32)
    mine = jnp.broadcast_to(jnp.sum(value * value, axis=1, keepdims=True), sq_mine.shape)
    sq_mine[...] = mine
    third = remote(sq_mine, sq_two, pair_send.at[2], pair_recv.at[2], twin)
    third.start()
    third.wait()
    inverse = lax.rsqrt((mine + sq_two[...])[:, :1] / width + 1e-06)
    normed = (value * inverse * gain_ref[...]).astype(jnp.bfloat16)
    rows = normed.shape[0] // 2
    everything[head, frame, 0] = normed[:rows]
    everything[head, frame, 1] = normed[rows:]
    copies = []

    def to_twin(source, half):
        slot = everything.at[head, source, half]
        copy = remote(slot, slot, twin_send.at[source, half], twin_recv.at[source, half], twin)
        copy.start()
        copies.append((copy, source, half))

    ring_start = [0]
    ring_gather(lambda source, half: everything.at[head, source, half], place, n,
                ring_send, ring_recv, to_twin)
    to_twin(frame, 0)
    to_twin(frame, 1)
    for copy, source, half in copies:
        copy.wait_send()
    for copy, source, half in copies:
        slot = everything.at[1 - head, source, half]
        remote(slot, slot, twin_send.at[source, half], twin_recv.at[source, half],
               twin).wait_recv()


def third_kernel(n, own_ref, other_ref, resid_ref, out_ref, twin_in, send_buf, recv_buf,
                 twin_send, twin_recv, ring_send, ring_recv):
    frame, head = lax.axis_index("frame"), lax.axis_index("head")
    place = ring_place(frame, n)
    twin = {"head": 1 - head}
    ends = [ring_frame((place + 1) % n, n), ring_frame((place + n - 1) % n, n)]
    far = n // 2
    greet([twin, {"frame": ends[0]}, {"frame": ends[1]}])
    schedule = [
        (step, way, half)
        for step in range(1, far + 1)
        for half in range(2)
        for way in range(2)
        if step > 1 or way == half
    ]

    def target(step, way):
        ahead = far + 1 - step
        return ring_frame((place + (ahead if way == 0 else n - ahead)) % n, n)

    twins = {}
    order = [(far, half) for half in range(2)]
    order = []
    for step, way, half in schedule:
        key = (1 if step == 1 else way, far + 1 - step, half)
        if key not in order:
            order.append(key)
    order += [(0, 0, 0), (0, 0, 1)]

    def frame_of(key):
        way, ahead, half = key
        return ring_frame((place + (ahead if way == 0 else n - ahead)) % n, n)

    for at, key in enumerate(order):
        q = frame_of(key)
        copy = remote(other_ref.at[q, key[2]], twin_in.at[q, key[2]], twin_send.at[at],
                      twin_recv.at[at], twin)
        copy.start()
        twins[key] = copy

    def term(key):
        twins[key].wait()
        q = frame_of(key)
        return own_ref[q, key[2]] + twin_in[q, key[2]].astype(jnp.float32)

    def arrival(step, way, half):
        slot = recv_buf.at[way, step - 1, half]
        remote(slot, slot, ring_send.at[way, step, half], ring_recv.at[way, step, half],
               {"frame": ends[way]}).wait_recv()
        return recv_buf[way, step - 1, half].astype(jnp.float32)

    started = []
    for step, way, half in schedule:
        key = (1 if step == 1 else way, far + 1 - step, half)
        total = term(key)
        if step > 2 or (step == 2 and way == half):
            total = total + arrival(step - 1, way, half)
        send_buf[way, step - 1, half] = total.astype(jnp.bfloat16)
        copy = remote(send_buf.at[way, step - 1, half], recv_buf.at[way, step - 1, half],
                      ring_send.at[way, step, half], ring_recv.at[way, step, half],
                      {"frame": ends[way]})
        copy.start()
        started.append(copy)
    rows = out_ref.shape[0] // 2
    for half in range(2):
        total = term((0, 0, half))
        for way in range(2):
            total = total + arrival(far, way, half)
        block = resid_ref[half * rows:(half + 1) * rows].astype(jnp.float32)
        out_ref[half * rows:(half + 1) * rows] = (block + total).astype(jnp.bfloat16)
    for copy in started:
        copy.wait_send()


VMEM = pl.BlockSpec(memory_space=pltpu.VMEM)


def call(kernel, ident, outs, scratch, *args):
    return pl.pallas_call(
        kernel,
        out_shape=outs,
        in_specs=[VMEM] * len(args),
        out_specs=[VMEM] * len(outs) if isinstance(outs, (list, tuple)) else VMEM,
        scratch_shapes=scratch,
        compiler_params=pltpu.CompilerParams(
            collective_id=ident, has_side_effects=True, vmem_limit_bytes=48 * 2**20
        ),
    )(*args)


def token_body(
    stream, queries, key_rows, value_rows, attn_gain, w_out, ffn_gain, w_up, conv_taps, w_down
):
    n = lax.axis_size("frame")
    frame, head = lax.axis_index("frame"), lax.axis_index("head")
    f32, bf16 = jnp.float32, jnp.bfloat16
    tokens = queries.shape[0]
    heads_here = queries.shape[1] // HEAD_DIM
    dma = pltpu.SemaphoreType.DMA
    far = n // 2
    ring = [dma((2, far + 1, 2)), dma((2, far + 1, 2))]

    def split(x):
        return x.reshape(tokens, heads_here, HEAD_DIM)

    pad = 128
    qpos = split(jnp.maximum(queries, 0))
    kpos = split(jnp.maximum(key_rows, 0))
    ones = jnp.zeros((tokens, heads_here, pad - HEAD_DIM), bf16).at[:, :, 0].set(1)
    values = jnp.concatenate([split(value_rows), ones], axis=2)
    own_state = jnp.einsum("thb,thc->hbc", kpos, values, preferred_element_type=f32)
    sent = own_state.astype(bf16).reshape(2, heads_here * HEAD_DIM // 2, pad)

    up_rows, hidden = w_up.shape
    part = hidden // n
    out_cols = w_down.shape[1]
    up_blocks = w_up.reshape(up_rows, n, part).transpose(1, 0, 2)
    down_blocks = w_down.reshape(n, part, out_cols)
    states, up_all, down_all = call(
        functools.partial(first_kernel, n), 0,
        [
            jax.ShapeDtypeStruct((n,) + sent.shape, bf16),
            jax.ShapeDtypeStruct((n, up_rows, part), bf16),
            jax.ShapeDtypeStruct((n, part, out_cols), bf16),
        ],
        [dma((3,))] + ring + [dma((2, n)), dma((2, n))],
        sent, up_blocks, down_blocks,
    )
    w_out_all = lax.all_gather(w_out, "frame", axis=1, tiled=True)
    earlier = (jnp.arange(n) < frame).astype(f32)
    state = own_state + jnp.sum(
        states.astype(f32) * earlier[:, None, None, None], axis=0
    ).reshape(own_state.shape)
    both = jnp.einsum(
        "thb,hbc->thc", qpos.astype(f32), state, precision=lax.Precision.HIGHEST
    )
    attended = both[:, :, :HEAD_DIM] / (both[:, :, HEAD_DIM:HEAD_DIM + 1] + 1e-06)
    attended = attended.reshape(tokens, heads_here * HEAD_DIM)
    squares = jnp.broadcast_to(
        jnp.sum(attended * attended, axis=1, keepdims=True), (tokens, 128)
    )
    gained = (attended * attn_gain).astype(bf16)
    width = stream.shape[1]
    half_out = [
        jnp.dot(gained, lax.dynamic_slice_in_dim(w_out_all, at * width, width, 1),
                preferred_element_type=f32)
        for at in (head, 1 - head)
    ]
    gain_here = lax.dynamic_slice_in_dim(ffn_gain, head * width, width, 0)[None]
    everything, resid = call(
        functools.partial(second_kernel, n, HEADS * HEAD_DIM, D), 1,
        [
            jax.ShapeDtypeStruct((2, n, 2, tokens // 2, width), bf16),
            jax.ShapeDtypeStruct((tokens, width), bf16),
        ],
        [
            pltpu.VMEM((tokens, width), f32),
            pltpu.VMEM((tokens, 128), f32),
            pltpu.VMEM((tokens, 128), f32),
            pltpu.VMEM((tokens, 128), f32),
            dma((3,)), dma((3,)),
        ] + ring + [dma((n, 2)), dma((n, 2))],
        half_out[0], half_out[1], squares, stream, gain_here,
    )
    ffn_in = everything.reshape(2, n * tokens, width)
    up_full = up_all.reshape(2, width, part)
    up_value = jnp.dot(ffn_in[0], up_full[0], preferred_element_type=f32) + jnp.dot(
        ffn_in[1], up_full[1], preferred_element_type=f32
    )
    hidden_all = jax.nn.silu(up_value).astype(bf16).reshape(n * tokens // TPF, TPF, part)
    padded = jnp.pad(hidden_all, ((1, 1), (0, 0), (0, 0))).astype(f32)
    taps = lax.dynamic_slice_in_dim(conv_taps, frame * part, part, 1)
    mixed = taps[0] * padded[:-2] + taps[1] * padded[1:-1] + taps[2] * padded[2:]
    mixed = mixed.astype(bf16).reshape(n * tokens, part)

    def down_half(at):
        blocks = lax.dynamic_slice_in_dim(down_all, at * (n // 2), n // 2, 0)
        return blocks.transpose(1, 0, 2).reshape(part, width)

    own = jnp.dot(mixed, down_half(head), preferred_element_type=f32)
    other = jnp.dot(mixed, down_half(1 - head), preferred_element_type=f32).astype(bf16)
    shape = (n, 2, tokens // 2, width)
    return call(
        functools.partial(third_kernel, n), 2,
        jax.ShapeDtypeStruct((tokens, width), bf16),
        [
            pltpu.VMEM(shape, bf16),
            pltpu.VMEM((2, far, 2, tokens // 2, width), bf16),
            pltpu.VMEM((2, far, 2, tokens // 2, width), bf16),
            dma((2 * n,)), dma((2 * n,)),
        ] + ring,
        own.reshape(shape), other.reshape(shape), resid,
    )


def solution(mesh):
    in_specs = (
        P(("groups", "frame"), "head"),
        P(("groups", "frame"), "head"),
        P(("groups", "frame"), "head"),
        P(("groups", "frame"), "head"),
        P("head"),
        P("head", "frame"),
        P(),
        P("frame", "head"),
        P(None, "head"),
        P("head", "frame"),
    )
    out_specs = P(("groups", "frame"), "head")
    frames, heads = mesh.shape["frame"], mesh.shape["head"]

    def step(*args):
        group_tokens = args[0].shape[0] // mesh.shape["groups"]
        width, hidden = args[7].shape
        tokens_move = (
            group_tokens <= hidden
            and heads == 2
            and frames % 2 == 0
            and frames >= 4
            and hidden % (heads * frames) == 0
            and width % (heads * frames) == 0
        )
        return jax.shard_map(
            token_body if tokens_move else body,
            mesh=mesh, in_specs=in_specs, out_specs=out_specs, check_vma=False,
        )(*args)

    return step
```

```python
import functools

import jax
import jax.numpy as jnp
from jax import lax
from jax.experimental import pallas as pl
from jax.experimental.pallas import tpu as pltpu
from jax.sharding import PartitionSpec as P

D = 2240
HEADS = 10
HEAD_DIM = 112
TPF = 128


def prefix(x, axis, combine, identity):
    length, place = (lax.axis_size(axis), lax.axis_index(axis))
    everything = jax.tree.map(lambda part: lax.all_gather(part, axis), x)
    start = jax.tree.map(
        lambda part, zero: jnp.broadcast_to(jnp.asarray(zero, part.dtype), part.shape), x, identity
    )

    def hop(k, before):
        reached = k < place
        new = combine(before, jax.tree.map(lambda part: part[k], everything))
        return jax.tree.map(lambda a, b: jnp.where(reached, a, b), new, before)

    return lax.fori_loop(0, length, hop, start)


def padded_2(block, sides, width):
    for axis, dim in sides:
        count = lax.axis_size(axis)
        forward = [(i, i + 1) for i in range(count - 1)]
        backward = [(target, source) for source, target in forward]
        low = lax.ppermute(
            lax.slice_in_dim(block, block.shape[dim] - width, None, axis=dim), axis, forward
        )
        high = lax.ppermute(lax.slice_in_dim(block, 0, width, axis=dim), axis, backward)
        block = jnp.concatenate([low, block, high], axis=dim)
    return block


def add_pair(earlier, later):
    return (earlier[0] + later[0], earlier[1] + later[1])


def body(
    stream, queries, key_rows, value_rows, attn_gain, w_out, ffn_gain, w_up, conv_taps, w_down
):
    highest = lax.Precision.HIGHEST
    tokens_here = queries.shape[0]
    frames_here = tokens_here // TPF
    heads_here = queries.shape[1] // HEAD_DIM
    qpos = jnp.maximum(queries.astype(jnp.float32), 0.0).reshape(
        frames_here, TPF, heads_here, HEAD_DIM
    )
    kpos = jnp.maximum(key_rows.astype(jnp.float32), 0.0).reshape(
        frames_here, TPF, heads_here, HEAD_DIM
    )
    values = value_rows.astype(jnp.float32).reshape(frames_here, TPF, heads_here, HEAD_DIM)
    frame_state = jnp.einsum("fthb,fthc->fhbc", kpos, values, precision=highest)
    frame_keys = jnp.sum(kpos, axis=1)
    own_state = jnp.sum(frame_state, axis=0)
    own_keys = jnp.sum(frame_keys, axis=0)
    empty_state = jnp.zeros_like(own_state)
    empty_keys = jnp.zeros_like(own_keys)
    before_state, before_keys = prefix(
        (own_state, own_keys), "frame", add_pair, (empty_state, empty_keys)
    )
    state = before_state[None] + jnp.cumsum(frame_state, axis=0)
    key_total = before_keys[None] + jnp.cumsum(frame_keys, axis=0)
    numer = jnp.einsum("fthb,fhbc->fthc", qpos, state, precision=highest)
    denom = jnp.einsum("fthb,fhb->fth", qpos, key_total, precision=highest) + 1e-06
    attended = (numer / denom[..., None]).reshape(tokens_here, heads_here * HEAD_DIM)
    squares = lax.psum(jnp.sum(attended * attended, axis=1), "head")
    scale = lax.rsqrt(squares / (HEADS * HEAD_DIM) + 1e-06)
    normed = (attended * scale[:, None] * attn_gain).astype(jnp.bfloat16)
    width_here = stream.shape[1]
    first_col = lax.axis_index("head") * width_here
    gain_here = lax.dynamic_slice_in_dim(ffn_gain, first_col, width_here, 0)
    proj = jnp.dot(
        normed,
        lax.all_gather(w_out, "frame", axis=1, tiled=True),
        preferred_element_type=jnp.float32,
    )
    proj_mine = lax.psum_scatter(proj, "head", scatter_dimension=1, tiled=True)
    resid_mine = (stream.astype(jnp.float32) + proj_mine).astype(jnp.bfloat16)
    resid_mine = lax.optimization_barrier(resid_mine)
    resid_float = resid_mine.astype(jnp.float32)
    total_sq = lax.psum(jnp.sum(resid_float * resid_float, axis=1), "head")
    inverse = lax.rsqrt(total_sq / D + 1e-06)
    normed_part = (resid_float * inverse[:, None] * gain_here).astype(jnp.bfloat16)
    ffn_in = lax.all_gather(normed_part, "head", axis=1, tiled=True)
    hidden_here = w_up.shape[1]
    up_value = jnp.dot(
        ffn_in,
        lax.all_gather(w_up, "frame", axis=0, tiled=True),
        preferred_element_type=jnp.float32,
    )
    hidden = (
        jax.nn.silu(up_value).astype(jnp.bfloat16).reshape(ffn_in.shape[0] // TPF, TPF, hidden_here)
    )
    padded = padded_2(hidden, (("frame", 0),), 1)
    padded_float = padded.astype(jnp.float32)
    mixed = (
        conv_taps[0] * padded_float[:-2]
        + conv_taps[1] * padded_float[1:-1]
        + conv_taps[2] * padded_float[2:]
    )
    mixed = mixed.astype(jnp.bfloat16).reshape(tokens_here, hidden_here)
    ffn_terms = jnp.dot(
        mixed,
        lax.all_gather(w_down, "frame", axis=1, tiled=True),
        preferred_element_type=jnp.float32,
    )
    ffn_mine = lax.psum_scatter(ffn_terms, "head", scatter_dimension=1, tiled=True)
    return (resid_float + ffn_mine).astype(jnp.bfloat16)


MESH_ID = pl.DeviceIdType.MESH


def ring_frame(pos, n):
    late = pos // (n // 2)
    return (1 - late) * (2 * pos) + late * (2 * (n - 1 - pos) + 1)


def ring_place(frame, n):
    odd = frame % 2
    return (1 - odd) * (frame // 2) + odd * (n - 1 - frame // 2)


def greet(partners):
    barrier = pltpu.get_barrier_semaphore()
    for partner in partners:
        pl.semaphore_signal(barrier, inc=1, device_id=partner, device_id_type=MESH_ID)
    pl.semaphore_wait(barrier, len(partners))


def remote(src, dst, send, recv, device):
    return pltpu.make_async_remote_copy(
        src_ref=src, dst_ref=dst, send_sem=send, recv_sem=recv,
        device_id=device, device_id_type=MESH_ID,
    )


def ring_steps(n):
    far = n // 2
    return [
        (step, way, half)
        for step in range(1, far + 1)
        for half in range(2)
        for way in range(2)
        if step < far or way == half
    ]


def ring_gather(buffer, place, n, send, recv, on_arrival):
    ends = [ring_frame((place + 1) % n, n), ring_frame((place + n - 1) % n, n)]
    started = []

    def origin(step, way):
        back = step if way == 0 else n - step
        return ring_frame((place + n - back) % n, n)

    def arrive(step, way, half):
        source = origin(step, way)
        slot = buffer(source, half)
        remote(slot, slot, send.at[way, step, half], recv.at[way, step, half],
               {"frame": ends[way]}).wait_recv()
        on_arrival(source, half)

    for step, way, half in ring_steps(n):
        if step > 1:
            arrive(step - 1, way, half)
        slot = buffer(origin(step - 1, way), half)
        copy = remote(slot, slot, send.at[way, step, half], recv.at[way, step, half],
                      {"frame": ends[way]})
        copy.start()
        started.append(copy)
    for step, way, half in ring_steps(n):
        last = n // 2 if way == half else n // 2 - 1
        if step == last:
            arrive(step, way, half)
    for copy in started:
        copy.wait_send()


def first_kernel(n, state_ref, up_ref, down_ref, proj_ref, states, weights, proj, blocks, here,
                 state_send, state_recv, proj_send, proj_recv, all_send, all_recv,
                 over_send, over_recv):
    frame, group = lax.axis_index("frame"), lax.axis_index("groups")
    place = ring_place(frame, n)
    over = {"groups": 1 - group}
    ends = [ring_frame((place + 1) % n, n), ring_frame((place + n - 1) % n, n)]
    far = n // 2
    part = weights.shape[3]
    local = [
        pltpu.make_async_copy(state_ref, states.at[frame], here.at[0]),
        pltpu.make_async_copy(proj_ref, proj.at[frame], here.at[1]),
    ]
    for copy in local:
        copy.start()
    for at, ref in enumerate((up_ref, down_ref)):
        for j in range(n):
            blocks[at, j] = ref[:, j * part:(j + 1) * part]
    for at in range(2):
        local.append(
            pltpu.make_async_copy(blocks.at[at, frame], weights.at[at, frame], here.at[2 + at])
        )
        local[-1].start()
    greet([{"frame": (frame + k) % n} for k in range(1, n)] + [over])
    local[0].wait()
    local[1].wait()

    def origin(step, way):
        back = step if way == 0 else n - step
        return ring_frame((place + n - back) % n, n)

    ring, pushed, swapped = [], [], []

    def state_copy(step, way, half, source):
        slot = states.at[source, half]
        return remote(slot, slot, state_send.at[way, step, half], state_recv.at[way, step, half],
                      {"frame": ends[way]})

    def proj_copy(step, way, source):
        slot = proj.at[source, group]
        return remote(slot, slot, proj_send.at[way, step], proj_recv.at[way, step],
                      {"frame": ends[way]})

    def swap(slot, at):
        copy = remote(slot, slot, over_send.at[at], over_recv.at[at], over)
        copy.start()
        swapped.append(copy)

    ways = list(range(1, n))
    ways.sort(key=lambda k: -min(k, n - k))
    for step in range(1, far + 1):
        for half in range(2):
            for way in range(2):
                if step == far and way != half:
                    continue
                if step > 1:
                    state_copy(step - 1, way, half, origin(step - 1, way)).wait_recv()
                copy = state_copy(step, way, half, origin(step - 1, way))
                copy.start()
                ring.append(copy)
        for way in range(2):
            if step > 1:
                source = origin(step - 1, way)
                proj_copy(step - 1, way, source).wait_recv()
            if step < far or way == 0:
                copy = proj_copy(step, way, origin(step - 1, way))
                copy.start()
                ring.append(copy)
            if step > 1:
                swap(proj.at[source, group], 2 * (step - 1) + way)
        for k in ways[2 * (step - 1):2 * step]:
            target = (frame + k) % n
            copy = remote(blocks.at[group, target], weights.at[group, frame], all_send.at[k],
                          all_recv.at[k], {"frame": target})
            copy.start()
            pushed.append(copy)
    for k in ways:
        source = (frame + n - k) % n
        slot = weights.at[group, source]
        remote(slot, slot, all_send.at[k], all_recv.at[k], {"frame": source}).wait_recv()
        swap(slot, 2 * far + k)
    proj_copy(far, 0, origin(far, 0)).wait_recv()
    swap(proj.at[origin(far, 0), group], 2 * far)
    for half in range(2):
        for way in range(2):
            last = far if way == half else far - 1
            state_copy(last, way, half, origin(last, way)).wait_recv()
    for copy in ring + pushed:
        copy.wait_send()

    def swapped_in(slot, at):
        remote(slot, slot, over_send.at[at], over_recv.at[at], over).wait_recv()

    for step in range(1, far):
        for way in range(2):
            swapped_in(proj.at[origin(step, way), 1 - group], 2 * step + way)
    swapped_in(proj.at[origin(far, 0), 1 - group], 2 * far)
    for k in ways:
        swapped_in(weights.at[1 - group, (frame + n - k) % n], 2 * far + k)
    for copy in swapped:
        copy.wait_send()
    local[2].wait()
    local[3].wait()


def second_kernel(n, features, width, own_ref, other_ref, sq_ref, stream_ref, gain_ref,
                  everything, resid, arrived, sq_in, sq_mine, sq_two,
                  pair_send, pair_recv, ring_send, ring_recv, twin_send, twin_recv):
    frame, head = lax.axis_index("frame"), lax.axis_index("head")
    place = ring_place(frame, n)
    twin = {"head": 1 - head}
    greet([twin, {"frame": ring_frame((place + 1) % n, n)},
           {"frame": ring_frame((place + n - 1) % n, n)}])
    first = remote(other_ref, arrived, pair_send.at[0], pair_recv.at[0], twin)
    second = remote(sq_ref, sq_in, pair_send.at[1], pair_recv.at[1], twin)
    second.start()
    first.start()
    second.wait()
    scale = lax.rsqrt((sq_ref[...] + sq_in[...])[:, :1] / features + 1e-06)
    first.wait()
    value = stream_ref[...].astype(jnp.float32) + (own_ref[...] + arrived[...]) * scale
    rounded = value.astype(jnp.bfloat16)
    resid[...] = rounded
    value = rounded.astype(jnp.float32)
    mine = jnp.broadcast_to(jnp.sum(value * value, axis=1, keepdims=True), sq_mine.shape)
    sq_mine[...] = mine
    third = remote(sq_mine, sq_two, pair_send.at[2], pair_recv.at[2], twin)
    third.start()
    third.wait()
    inverse = lax.rsqrt((mine + sq_two[...])[:, :1] / width + 1e-06)
    normed = (value * inverse * gain_ref[...]).astype(jnp.bfloat16)
    rows = normed.shape[0] // 2
    everything[head, frame, 0] = normed[:rows]
    everything[head, frame, 1] = normed[rows:]
    copies = []

    def to_twin(source, half):
        slot = everything.at[head, source, half]
        copy = remote(slot, slot, twin_send.at[source, half], twin_recv.at[source, half], twin)
        copy.start()
        copies.append((copy, source, half))

    ring_start = [0]
    ring_gather(lambda source, half: everything.at[head, source, half], place, n,
                ring_send, ring_recv, to_twin)
    to_twin(frame, 0)
    to_twin(frame, 1)
    for copy, source, half in copies:
        copy.wait_send()
    for copy, source, half in copies:
        slot = everything.at[1 - head, source, half]
        remote(slot, slot, twin_send.at[source, half], twin_recv.at[source, half],
               twin).wait_recv()


def third_kernel(n, own_ref, other_ref, resid_ref, out_ref, twin_in, send_buf, recv_buf,
                 twin_send, twin_recv, ring_send, ring_recv):
    frame, head = lax.axis_index("frame"), lax.axis_index("head")
    place = ring_place(frame, n)
    twin = {"head": 1 - head}
    ends = [ring_frame((place + 1) % n, n), ring_frame((place + n - 1) % n, n)]
    far = n // 2
    greet([twin, {"frame": ends[0]}, {"frame": ends[1]}])
    schedule = [
        (step, way, half)
        for step in range(1, far + 1)
        for half in range(2)
        for way in range(2)
        if step > 1 or way == half
    ]

    def target(step, way):
        ahead = far + 1 - step
        return ring_frame((place + (ahead if way == 0 else n - ahead)) % n, n)

    twins = {}
    order = [(far, half) for half in range(2)]
    order = []
    for step, way, half in schedule:
        key = (1 if step == 1 else way, far + 1 - step, half)
        if key not in order:
            order.append(key)
    order += [(0, 0, 0), (0, 0, 1)]

    def frame_of(key):
        way, ahead, half = key
        return ring_frame((place + (ahead if way == 0 else n - ahead)) % n, n)

    for at, key in enumerate(order):
        q = frame_of(key)
        copy = remote(other_ref.at[q, key[2]], twin_in.at[q, key[2]], twin_send.at[at],
                      twin_recv.at[at], twin)
        copy.start()
        twins[key] = copy

    def term(key):
        twins[key].wait()
        q = frame_of(key)
        return own_ref[q, key[2]] + twin_in[q, key[2]].astype(jnp.float32)

    def arrival(step, way, half):
        slot = recv_buf.at[way, step - 1, half]
        remote(slot, slot, ring_send.at[way, step, half], ring_recv.at[way, step, half],
               {"frame": ends[way]}).wait_recv()
        return recv_buf[way, step - 1, half].astype(jnp.float32)

    started = []
    for step, way, half in schedule:
        key = (1 if step == 1 else way, far + 1 - step, half)
        total = term(key)
        if step > 2 or (step == 2 and way == half):
            total = total + arrival(step - 1, way, half)
        send_buf[way, step - 1, half] = total.astype(jnp.bfloat16)
        copy = remote(send_buf.at[way, step - 1, half], recv_buf.at[way, step - 1, half],
                      ring_send.at[way, step, half], ring_recv.at[way, step, half],
                      {"frame": ends[way]})
        copy.start()
        started.append(copy)
    rows = out_ref.shape[0] // 2
    for half in range(2):
        total = term((0, 0, half))
        for way in range(2):
            total = total + arrival(far, way, half)
        block = resid_ref[half * rows:(half + 1) * rows].astype(jnp.float32)
        out_ref[half * rows:(half + 1) * rows] = (block + total).astype(jnp.bfloat16)
    for copy in started:
        copy.wait_send()


VMEM = pl.BlockSpec(memory_space=pltpu.VMEM)


def call(kernel, ident, outs, scratch, *args):
    return pl.pallas_call(
        kernel,
        out_shape=outs,
        in_specs=[VMEM] * len(args),
        out_specs=[VMEM] * len(outs) if isinstance(outs, (list, tuple)) else VMEM,
        scratch_shapes=scratch,
        compiler_params=pltpu.CompilerParams(
            collective_id=ident, has_side_effects=True, vmem_limit_bytes=48 * 2**20
        ),
    )(*args)


def token_body(
    stream, queries, key_rows, value_rows, attn_gain, w_out, ffn_gain, w_up, conv_taps, w_down
):
    n = lax.axis_size("frame")
    frame, head = lax.axis_index("frame"), lax.axis_index("head")
    f32, bf16 = jnp.float32, jnp.bfloat16
    tokens = queries.shape[0]
    heads_here = queries.shape[1] // HEAD_DIM
    dma = pltpu.SemaphoreType.DMA
    far = n // 2
    ring = [dma((2, far + 1, 2)), dma((2, far + 1, 2))]

    def split(x):
        return x.reshape(tokens, heads_here, HEAD_DIM)

    pad = 128
    qpos = split(jnp.maximum(queries, 0))
    kpos = split(jnp.maximum(key_rows, 0))
    ones = jnp.zeros((tokens, heads_here, pad - HEAD_DIM), bf16).at[:, :, 0].set(1)
    values = jnp.concatenate([split(value_rows), ones], axis=2)
    own_state = jnp.einsum("thb,thc->hbc", kpos, values, preferred_element_type=f32)
    sent = own_state.astype(bf16).reshape(2, heads_here * HEAD_DIM // 2, pad)

    up_rows, hidden = w_up.shape
    part = hidden // n
    out_cols = w_down.shape[1]
    states, weights, proj = call(
        functools.partial(first_kernel, n), 0,
        [
            jax.ShapeDtypeStruct((n,) + sent.shape, bf16),
            jax.ShapeDtypeStruct((2, n, up_rows, part), bf16),
            jax.ShapeDtypeStruct((n, 2, out_cols // 2, w_out.shape[0]), bf16),
        ],
        [pltpu.VMEM((2, n, up_rows, part), bf16), dma((4,))] + ring
        + [dma((2, far + 1)), dma((2, far + 1)), dma((n,)), dma((n,)), dma((2 * n,)), dma((2 * n,))],
        sent, w_up, w_down.T, w_out.T.reshape(2, out_cols // 2, w_out.shape[0]),
    )
    up_all, down_all = weights[0], weights[1]
    proj_t = proj.reshape(n * out_cols, w_out.shape[0])
    earlier = (jnp.arange(n) < frame).astype(f32)
    state = own_state + jnp.sum(
        states.astype(f32) * earlier[:, None, None, None], axis=0
    ).reshape(own_state.shape)
    both = jnp.einsum(
        "thb,hbc->thc", qpos.astype(f32), state, precision=lax.Precision.HIGHEST
    )
    attended = both[:, :, :HEAD_DIM] / (both[:, :, HEAD_DIM:HEAD_DIM + 1] + 1e-06)
    attended = attended.reshape(tokens, heads_here * HEAD_DIM)
    squares = jnp.broadcast_to(
        jnp.sum(attended * attended, axis=1, keepdims=True), (tokens, 128)
    )
    gained = (attended * attn_gain).astype(bf16)
    width = stream.shape[1]
    def against(x, y):
        return lax.dot_general(x, y, (((1,), (1,)), ((), ())), preferred_element_type=f32)

    half_out = [
        against(gained, lax.dynamic_slice_in_dim(proj_t, at * width, width, 0))
        for at in (head, 1 - head)
    ]
    gain_here = lax.dynamic_slice_in_dim(ffn_gain, head * width, width, 0)[None]
    everything, resid = call(
        functools.partial(second_kernel, n, HEADS * HEAD_DIM, D), 1,
        [
            jax.ShapeDtypeStruct((2, n, 2, tokens // 2, width), bf16),
            jax.ShapeDtypeStruct((tokens, width), bf16),
        ],
        [
            pltpu.VMEM((tokens, width), f32),
            pltpu.VMEM((tokens, 128), f32),
            pltpu.VMEM((tokens, 128), f32),
            pltpu.VMEM((tokens, 128), f32),
            dma((3,)), dma((3,)),
        ] + ring + [dma((n, 2)), dma((n, 2))],
        half_out[0], half_out[1], squares, stream, gain_here,
    )
    ffn_in = everything.reshape(2, n * tokens, width)
    up_full = up_all.reshape(2, width, part)
    up_value = jnp.dot(ffn_in[0], up_full[0], preferred_element_type=f32) + jnp.dot(
        ffn_in[1], up_full[1], preferred_element_type=f32
    )
    hidden_all = jax.nn.silu(up_value).astype(bf16).reshape(n * tokens // TPF, TPF, part)
    padded = jnp.pad(hidden_all, ((1, 1), (0, 0), (0, 0))).astype(f32)
    taps = lax.dynamic_slice_in_dim(conv_taps, frame * part, part, 1)
    mixed = taps[0] * padded[:-2] + taps[1] * padded[1:-1] + taps[2] * padded[2:]
    mixed = mixed.astype(bf16).reshape(n * tokens, part)

    def down_half(at):
        return against(
            mixed, lax.dynamic_slice_in_dim(down_all, at * (n // 2), n // 2, 0).reshape(width, part)
        )

    own = down_half(head)
    other = down_half(1 - head).astype(bf16)
    shape = (n, 2, tokens // 2, width)
    return call(
        functools.partial(third_kernel, n), 2,
        jax.ShapeDtypeStruct((tokens, width), bf16),
        [
            pltpu.VMEM(shape, bf16),
            pltpu.VMEM((2, far, 2, tokens // 2, width), bf16),
            pltpu.VMEM((2, far, 2, tokens // 2, width), bf16),
            dma((2 * n,)), dma((2 * n,)),
        ] + ring,
        own.reshape(shape), other.reshape(shape), resid,
    )


def solution(mesh):
    in_specs = (
        P(("groups", "frame"), "head"),
        P(("groups", "frame"), "head"),
        P(("groups", "frame"), "head"),
        P(("groups", "frame"), "head"),
        P("head"),
        P("head", "frame"),
        P(),
        P("frame", "head"),
        P(None, "head"),
        P("head", "frame"),
    )
    out_specs = P(("groups", "frame"), "head")
    frames, heads = mesh.shape["frame"], mesh.shape["head"]

    def step(*args):
        group_tokens = args[0].shape[0] // mesh.shape["groups"]
        width, hidden = args[7].shape
        tokens_move = (
            group_tokens <= hidden
            and heads == 2
            and mesh.shape["groups"] == 2
            and frames % 2 == 0
            and frames >= 4
            and hidden % (heads * frames) == 0
            and width % (heads * frames) == 0
            and args[5].shape[1] % (2 * frames) == 0
        )
        return jax.shard_map(
            token_body if tokens_move else body,
            mesh=mesh, in_specs=in_specs, out_specs=out_specs, check_vma=False,
        )(*args)

    return step
```

```python
import functools

import jax
import jax.numpy as jnp
from jax import lax
from jax.experimental import pallas as pl
from jax.experimental.pallas import tpu as pltpu
from jax.sharding import PartitionSpec as P

D = 2240
HEADS = 10
HEAD_DIM = 112
TPF = 128


def prefix(x, axis, combine, identity):
    length, place = (lax.axis_size(axis), lax.axis_index(axis))
    everything = jax.tree.map(lambda part: lax.all_gather(part, axis), x)
    start = jax.tree.map(
        lambda part, zero: jnp.broadcast_to(jnp.asarray(zero, part.dtype), part.shape), x, identity
    )

    def hop(k, before):
        reached = k < place
        new = combine(before, jax.tree.map(lambda part: part[k], everything))
        return jax.tree.map(lambda a, b: jnp.where(reached, a, b), new, before)

    return lax.fori_loop(0, length, hop, start)


def padded_2(block, sides, width):
    for axis, dim in sides:
        count = lax.axis_size(axis)
        forward = [(i, i + 1) for i in range(count - 1)]
        backward = [(target, source) for source, target in forward]
        low = lax.ppermute(
            lax.slice_in_dim(block, block.shape[dim] - width, None, axis=dim), axis, forward
        )
        high = lax.ppermute(lax.slice_in_dim(block, 0, width, axis=dim), axis, backward)
        block = jnp.concatenate([low, block, high], axis=dim)
    return block


def add_pair(earlier, later):
    return (earlier[0] + later[0], earlier[1] + later[1])


def body(
    stream, queries, key_rows, value_rows, attn_gain, w_out, ffn_gain, w_up, conv_taps, w_down
):
    highest = lax.Precision.HIGHEST
    tokens_here = queries.shape[0]
    frames_here = tokens_here // TPF
    heads_here = queries.shape[1] // HEAD_DIM
    qpos = jnp.maximum(queries.astype(jnp.float32), 0.0).reshape(
        frames_here, TPF, heads_here, HEAD_DIM
    )
    kpos = jnp.maximum(key_rows.astype(jnp.float32), 0.0).reshape(
        frames_here, TPF, heads_here, HEAD_DIM
    )
    values = value_rows.astype(jnp.float32).reshape(frames_here, TPF, heads_here, HEAD_DIM)
    frame_state = jnp.einsum("fthb,fthc->fhbc", kpos, values, precision=highest)
    frame_keys = jnp.sum(kpos, axis=1)
    own_state = jnp.sum(frame_state, axis=0)
    own_keys = jnp.sum(frame_keys, axis=0)
    empty_state = jnp.zeros_like(own_state)
    empty_keys = jnp.zeros_like(own_keys)
    before_state, before_keys = prefix(
        (own_state, own_keys), "frame", add_pair, (empty_state, empty_keys)
    )
    state = before_state[None] + jnp.cumsum(frame_state, axis=0)
    key_total = before_keys[None] + jnp.cumsum(frame_keys, axis=0)
    numer = jnp.einsum("fthb,fhbc->fthc", qpos, state, precision=highest)
    denom = jnp.einsum("fthb,fhb->fth", qpos, key_total, precision=highest) + 1e-06
    attended = (numer / denom[..., None]).reshape(tokens_here, heads_here * HEAD_DIM)
    squares = lax.psum(jnp.sum(attended * attended, axis=1), "head")
    scale = lax.rsqrt(squares / (HEADS * HEAD_DIM) + 1e-06)
    normed = (attended * scale[:, None] * attn_gain).astype(jnp.bfloat16)
    width_here = stream.shape[1]
    first_col = lax.axis_index("head") * width_here
    gain_here = lax.dynamic_slice_in_dim(ffn_gain, first_col, width_here, 0)
    proj = jnp.dot(
        normed,
        lax.all_gather(w_out, "frame", axis=1, tiled=True),
        preferred_element_type=jnp.float32,
    )
    proj_mine = lax.psum_scatter(proj, "head", scatter_dimension=1, tiled=True)
    resid_mine = (stream.astype(jnp.float32) + proj_mine).astype(jnp.bfloat16)
    resid_mine = lax.optimization_barrier(resid_mine)
    resid_float = resid_mine.astype(jnp.float32)
    total_sq = lax.psum(jnp.sum(resid_float * resid_float, axis=1), "head")
    inverse = lax.rsqrt(total_sq / D + 1e-06)
    normed_part = (resid_float * inverse[:, None] * gain_here).astype(jnp.bfloat16)
    ffn_in = lax.all_gather(normed_part, "head", axis=1, tiled=True)
    hidden_here = w_up.shape[1]
    up_value = jnp.dot(
        ffn_in,
        lax.all_gather(w_up, "frame", axis=0, tiled=True),
        preferred_element_type=jnp.float32,
    )
    hidden = (
        jax.nn.silu(up_value).astype(jnp.bfloat16).reshape(ffn_in.shape[0] // TPF, TPF, hidden_here)
    )
    padded = padded_2(hidden, (("frame", 0),), 1)
    padded_float = padded.astype(jnp.float32)
    mixed = (
        conv_taps[0] * padded_float[:-2]
        + conv_taps[1] * padded_float[1:-1]
        + conv_taps[2] * padded_float[2:]
    )
    mixed = mixed.astype(jnp.bfloat16).reshape(tokens_here, hidden_here)
    ffn_terms = jnp.dot(
        mixed,
        lax.all_gather(w_down, "frame", axis=1, tiled=True),
        preferred_element_type=jnp.float32,
    )
    ffn_mine = lax.psum_scatter(ffn_terms, "head", scatter_dimension=1, tiled=True)
    return (resid_float + ffn_mine).astype(jnp.bfloat16)


MESH_ID = pl.DeviceIdType.MESH


def ring_frame(pos, n):
    late = pos // (n // 2)
    return (1 - late) * (2 * pos) + late * (2 * (n - 1 - pos) + 1)


def ring_place(frame, n):
    odd = frame % 2
    return (1 - odd) * (frame // 2) + odd * (n - 1 - frame // 2)


def greet(partners):
    barrier = pltpu.get_barrier_semaphore()
    for partner in partners:
        pl.semaphore_signal(barrier, inc=1, device_id=partner, device_id_type=MESH_ID)
    pl.semaphore_wait(barrier, len(partners))


def remote(src, dst, send, recv, device):
    return pltpu.make_async_remote_copy(
        src_ref=src, dst_ref=dst, send_sem=send, recv_sem=recv,
        device_id=device, device_id_type=MESH_ID,
    )


def ring_steps(n):
    far = n // 2
    return [
        (step, way, half)
        for step in range(1, far + 1)
        for half in range(2)
        for way in range(2)
        if step < far or way == half
    ]


def ring_gather(buffer, place, n, send, recv, on_arrival, after_step):
    ends = [ring_frame((place + 1) % n, n), ring_frame((place + n - 1) % n, n)]
    started = []

    def origin(step, way):
        back = step if way == 0 else n - step
        return ring_frame((place + n - back) % n, n)

    def arrive(step, way, half):
        source = origin(step, way)
        slot = buffer(source, half)
        remote(slot, slot, send.at[way, step, half], recv.at[way, step, half],
               {"frame": ends[way]}).wait_recv()
        on_arrival(source, half)

    for step, way, half in ring_steps(n):
        if step > 1:
            arrive(step - 1, way, half)
        slot = buffer(origin(step - 1, way), half)
        copy = remote(slot, slot, send.at[way, step, half], recv.at[way, step, half],
                      {"frame": ends[way]})
        copy.start()
        started.append(copy)
        if way == 1 and half == 1:
            if step == n // 2:
                arrive(step - 1, 0, 1)
                arrive(step - 1, 1, 0)
            after_step([ring_frame(place, n)] if step == 1 else
                       [origin(step - 1, 0), origin(step - 1, 1)])
    for way in range(2):
        arrive(n // 2, way, way)
    after_step([origin(n // 2, 0)])
    return started


def first_kernel(n, state_ref, up_ref, down_ref, proj_ref, states, weights, merged, proj,
                 blocks, here,
                 state_send, state_recv, proj_send, proj_recv, all_send, all_recv,
                 over_send, over_recv):
    frame, group = lax.axis_index("frame"), lax.axis_index("groups")
    place = ring_place(frame, n)
    over = {"groups": 1 - group}
    ends = [ring_frame((place + 1) % n, n), ring_frame((place + n - 1) % n, n)]
    far = n // 2
    part = weights.shape[3]
    local = [
        pltpu.make_async_copy(state_ref, states.at[frame], here.at[0]),
        pltpu.make_async_copy(proj_ref, proj.at[frame], here.at[1]),
    ]
    for copy in local:
        copy.start()
    for at, ref in enumerate((up_ref, down_ref)):
        for j in range(n):
            blocks[at, j] = ref[:, j * part:(j + 1) * part]
    for at in range(2):
        local.append(
            pltpu.make_async_copy(blocks.at[at, frame], weights.at[at, frame], here.at[2 + at])
        )
        local[-1].start()
    greet([{"frame": (frame + k) % n} for k in range(1, n)] + [over])
    local[0].wait()
    local[1].wait()

    def origin(step, way):
        back = step if way == 0 else n - step
        return ring_frame((place + n - back) % n, n)

    ring, pushed, swapped = [], [], []

    def state_copy(step, way, half, source):
        slot = states.at[source, half]
        return remote(slot, slot, state_send.at[way, step, half], state_recv.at[way, step, half],
                      {"frame": ends[way]})

    def proj_copy(step, way, source):
        slot = proj.at[source, group]
        return remote(slot, slot, proj_send.at[way, step], proj_recv.at[way, step],
                      {"frame": ends[way]})

    def swap(slot, at):
        copy = remote(slot, slot, over_send.at[at], over_recv.at[at], over)
        copy.start()
        swapped.append(copy)

    ways = list(range(1, n))
    ways.sort(key=lambda k: -min(k, n - k))
    for step in range(1, far + 1):
        for half in range(2):
            for way in range(2):
                if step == far and way != half:
                    continue
                if step > 1:
                    state_copy(step - 1, way, half, origin(step - 1, way)).wait_recv()
                copy = state_copy(step, way, half, origin(step - 1, way))
                copy.start()
                ring.append(copy)
        for way in range(2):
            if step > 1:
                source = origin(step - 1, way)
                proj_copy(step - 1, way, source).wait_recv()
            if step < far or way == 0:
                copy = proj_copy(step, way, origin(step - 1, way))
                copy.start()
                ring.append(copy)
            if step > 1:
                swap(proj.at[source, group], 2 * (step - 1) + way)
        for k in ways[2 * (step - 1):2 * step]:
            target = (frame + k) % n
            copy = remote(blocks.at[group, target], weights.at[group, frame], all_send.at[k],
                          all_recv.at[k], {"frame": target})
            copy.start()
            pushed.append(copy)
    for k in ways:
        source = (frame + n - k) % n
        slot = weights.at[group, source]
        remote(slot, slot, all_send.at[k], all_recv.at[k], {"frame": source}).wait_recv()
        swap(slot, 2 * far + k)
    proj_copy(far, 0, origin(far, 0)).wait_recv()
    swap(proj.at[origin(far, 0), group], 2 * far)
    for half in range(2):
        for way in range(2):
            last = far if way == half else far - 1
            state_copy(last, way, half, origin(last, way)).wait_recv()
    for copy in ring + pushed:
        copy.wait_send()

    def swapped_in(slot, at):
        remote(slot, slot, over_send.at[at], over_recv.at[at], over).wait_recv()

    for step in range(1, far):
        for way in range(2):
            swapped_in(proj.at[origin(step, way), 1 - group], 2 * step + way)
    swapped_in(proj.at[origin(far, 0), 1 - group], 2 * far)
    count = proj.shape[2]
    for at in range(n):
        for half in range(2):
            first_row = (2 * at + half) * count
            merged[first_row:first_row + count] = proj[at, half]
    for k in ways:
        swapped_in(weights.at[1 - group, (frame + n - k) % n], 2 * far + k)
    for copy in swapped:
        copy.wait_send()
    local[2].wait()
    local[3].wait()


def second_kernel(n, features, width, own_ref, other_ref, sq_ref, stream_ref, gain_ref,
                  up_ref, down_ref, taps_ref, out_ref,
                  everything, resid, arrived, sq_in, sq_mine, sq_two, hidden, mixed, theirs,
                  twin_in, send_buf, recv_buf,
                  pair_send, pair_recv, ring_send, ring_recv, twin_send, twin_recv,
                  sum_twin_send, sum_twin_recv, sum_send, sum_recv):
    frame, head = lax.axis_index("frame"), lax.axis_index("head")
    place = ring_place(frame, n)
    twin = {"head": 1 - head}
    ends = [ring_frame((place + 1) % n, n), ring_frame((place + n - 1) % n, n)]
    far = n // 2
    rows = stream_ref.shape[0] // 2
    hidden[0] = jnp.zeros_like(hidden[0])
    hidden[n + 1] = jnp.zeros_like(hidden[0])
    greet([twin, {"frame": ends[0]}, {"frame": ends[1]}])
    first = remote(other_ref, arrived, pair_send.at[0], pair_recv.at[0], twin)
    second = remote(sq_ref, sq_in, pair_send.at[1], pair_recv.at[1], twin)
    second.start()
    first.start()
    second.wait()
    scale = lax.rsqrt((sq_ref[...] + sq_in[...])[:, :1] / features + 1e-06)
    first.wait()
    value = stream_ref[...].astype(jnp.float32) + (own_ref[...] + arrived[...]) * scale
    rounded = value.astype(jnp.bfloat16)
    resid[...] = rounded
    value = rounded.astype(jnp.float32)
    mine = jnp.broadcast_to(jnp.sum(value * value, axis=1, keepdims=True), sq_mine.shape)
    sq_mine[...] = mine
    third = remote(sq_mine, sq_two, pair_send.at[2], pair_recv.at[2], twin)
    third.start()
    third.wait()
    inverse = lax.rsqrt((mine + sq_two[...])[:, :1] / width + 1e-06)
    normed = (value * inverse * gain_ref[...]).astype(jnp.bfloat16)
    everything[head, frame, 0] = normed[:rows]
    everything[head, frame, 1] = normed[rows:]
    copies = []

    def to_twin(source, half):
        slot = everything.at[head, source, half]
        copy = remote(slot, slot, twin_send.at[source, half], twin_recv.at[source, half], twin)
        copy.start()
        copies.append(copy)

    def up_blocks(sources):
        for source in sources:
            for half in range(2):
                slot = everything.at[1 - head, source, half]
                remote(slot, slot, twin_send.at[source, half], twin_recv.at[source, half],
                       twin).wait_recv()
            total = None
            for at in range(2):
                block = jnp.concatenate(
                    [everything[at, source, 0], everything[at, source, 1]], axis=0
                )
                term = jnp.dot(block, up_ref[at], preferred_element_type=jnp.float32)
                total = term if total is None else total + term
            act = total / (1.0 + jnp.exp(-total))
            hidden[source + 1] = act.astype(jnp.bfloat16).astype(jnp.float32)

    to_twin(frame, 0)
    to_twin(frame, 1)
    gathers = ring_gather(lambda source, half: everything.at[head, source, half], place, n,
                          ring_send, ring_recv, to_twin, up_blocks)

    def frame_of(way, ahead):
        return ring_frame((place + (ahead if way == 0 else n - ahead)) % n, n)

    twins = {}

    def produce(way, ahead):
        q = frame_of(way, ahead)
        blend = (
            taps_ref[0:1] * hidden[q] + taps_ref[1:2] * hidden[q + 1]
            + taps_ref[2:3] * hidden[q + 2]
        ).astype(jnp.bfloat16)
        mixed[q] = blend
        product = against(blend, down_ref[1 - head]).astype(jnp.bfloat16)
        for half in range(2):
            theirs[q, half] = product[half * rows:(half + 1) * rows]
            at = len(twins)
            copy = remote(theirs.at[q, half], twin_in.at[q, half], sum_twin_send.at[at],
                          sum_twin_recv.at[at], twin)
            copy.start()
            twins[way, ahead, half] = copy

    def produce_step(step):
        ahead = far + 1 - step
        produce(1, ahead)
        if 0 < ahead < far:
            produce(0, ahead)

    def terms(way, ahead):
        q = frame_of(way, ahead)
        own = against(mixed[q], down_ref[head])
        out = []
        for half in range(2):
            twins[way, ahead, half].wait()
            out.append(own[half * rows:(half + 1) * rows]
                       + twin_in[q, half].astype(jnp.float32))
        return out

    def arrival(step, way, half):
        slot = recv_buf.at[way, step - 1, half]
        remote(slot, slot, sum_send.at[way, step, half], sum_recv.at[way, step, half],
               {"frame": ends[way]}).wait_recv()
        return recv_buf[way, step - 1, half].astype(jnp.float32)

    started = []

    def send_sum(step, way, half, total):
        if step > 2 or (step == 2 and way == half):
            total = total + arrival(step - 1, way, half)
        send_buf[way, step - 1, half] = total.astype(jnp.bfloat16)
        copy = remote(send_buf.at[way, step - 1, half], recv_buf.at[way, step - 1, half],
                      sum_send.at[way, step, half], sum_recv.at[way, step, half],
                      {"frame": ends[way]})
        copy.start()
        started.append(copy)

    produce_step(1)
    produce_step(2)
    for step in range(1, far + 1):
        ahead = far + 1 - step
        if step == 1:
            held = terms(1, ahead)
            send_sum(1, 0, 0, held[0])
            send_sum(1, 1, 1, held[1])
        else:
            held = [terms(0, ahead), terms(1, ahead)]
            for half in range(2):
                for way in range(2):
                    send_sum(step, way, half, held[way][half])
        if step < far:
            produce_step(step + 2)
    held = terms(1, 0)
    for half in range(2):
        total = held[half]
        for way in range(2):
            total = total + arrival(far, way, half)
        block = resid[half * rows:(half + 1) * rows].astype(jnp.float32)
        out_ref[half * rows:(half + 1) * rows] = (block + total).astype(jnp.bfloat16)
    for copy in started + copies + gathers:
        copy.wait_send()


def against(x, y):
    return lax.dot_general(x, y, (((1,), (1,)), ((), ())), preferred_element_type=jnp.float32)


VMEM = pl.BlockSpec(memory_space=pltpu.VMEM)


def call(kernel, ident, outs, scratch, *args):
    return pl.pallas_call(
        kernel,
        out_shape=outs,
        in_specs=[VMEM] * len(args),
        out_specs=[VMEM] * len(outs) if isinstance(outs, (list, tuple)) else VMEM,
        scratch_shapes=scratch,
        compiler_params=pltpu.CompilerParams(
            collective_id=ident, has_side_effects=True, vmem_limit_bytes=48 * 2**20
        ),
    )(*args)


def token_body(
    stream, queries, key_rows, value_rows, attn_gain, w_out, ffn_gain, w_up, conv_taps, w_down
):
    n = lax.axis_size("frame")
    frame, head = lax.axis_index("frame"), lax.axis_index("head")
    f32, bf16 = jnp.float32, jnp.bfloat16
    tokens = queries.shape[0]
    heads_here = queries.shape[1] // HEAD_DIM
    dma = pltpu.SemaphoreType.DMA
    far = n // 2
    ring = [dma((2, far + 1, 2)), dma((2, far + 1, 2))]

    def split(x):
        return x.reshape(tokens, heads_here, HEAD_DIM)

    pad = 128
    qpos = split(jnp.maximum(queries, 0))
    kpos = split(jnp.maximum(key_rows, 0))
    ones = jnp.zeros((tokens, heads_here, pad - HEAD_DIM), bf16).at[:, :, 0].set(1)
    values = jnp.concatenate([split(value_rows), ones], axis=2)
    own_state = jnp.einsum("thb,thc->hbc", kpos, values, preferred_element_type=f32)
    sent = own_state.astype(bf16).reshape(2, heads_here * HEAD_DIM // 2, pad)

    up_rows, hidden = w_up.shape
    part = hidden // n
    out_cols = w_down.shape[1]
    states, weights, proj_t = call(
        functools.partial(first_kernel, n), 0,
        [
            jax.ShapeDtypeStruct((n,) + sent.shape, bf16),
            jax.ShapeDtypeStruct((2, n, up_rows, part), bf16),
            jax.ShapeDtypeStruct((n * out_cols, w_out.shape[0]), bf16),
        ],
        [pltpu.VMEM((n, 2, out_cols // 2, w_out.shape[0]), bf16),
         pltpu.VMEM((2, n, up_rows, part), bf16), dma((4,))] + ring
        + [dma((2, far + 1)), dma((2, far + 1)), dma((n,)), dma((n,)), dma((2 * n,)), dma((2 * n,))],
        sent, w_up, w_down.T, w_out.T.reshape(2, out_cols // 2, w_out.shape[0]),
    )
    earlier = (jnp.arange(n) < frame).astype(f32)
    state = own_state + jnp.sum(
        states.astype(f32) * earlier[:, None, None, None], axis=0
    ).reshape(own_state.shape)
    both = jnp.einsum(
        "thb,hbc->thc", qpos.astype(f32), state, precision=lax.Precision.HIGHEST
    )
    attended = both[:, :, :HEAD_DIM] / (both[:, :, HEAD_DIM:HEAD_DIM + 1] + 1e-06)
    attended = attended.reshape(tokens, heads_here * HEAD_DIM)
    squares = jnp.broadcast_to(
        jnp.sum(attended * attended, axis=1, keepdims=True), (tokens, 128)
    )
    gained = (attended * attn_gain).astype(bf16)
    width = stream.shape[1]
    half_out = [
        against(gained, lax.dynamic_slice_in_dim(proj_t, at * width, width, 0))
        for at in (head, 1 - head)
    ]
    gain_here = lax.dynamic_slice_in_dim(ffn_gain, head * width, width, 0)[None]
    taps = lax.dynamic_slice_in_dim(conv_taps, frame * part, part, 1)
    both_weights = weights.reshape(2, 2, width, part)
    shape = (n, 2, tokens // 2, width)
    link = (2, far, 2, tokens // 2, width)
    return call(
        functools.partial(second_kernel, n, HEADS * HEAD_DIM, D), 1,
        jax.ShapeDtypeStruct((tokens, width), bf16),
        [
            pltpu.VMEM((2,) + shape, bf16),
            pltpu.VMEM((tokens, width), bf16),
            pltpu.VMEM((tokens, width), f32),
            pltpu.VMEM((tokens, 128), f32),
            pltpu.VMEM((tokens, 128), f32),
            pltpu.VMEM((tokens, 128), f32),
            pltpu.VMEM((n + 2, tokens, part), f32),
            pltpu.VMEM((n, tokens, part), bf16),
            pltpu.VMEM(shape, bf16),
            pltpu.VMEM(shape, bf16),
            pltpu.VMEM(link, bf16),
            pltpu.VMEM(link, bf16),
            dma((3,)), dma((3,)),
        ] + ring + [dma((n, 2)), dma((n, 2)), dma((2 * n,)), dma((2 * n,))] + ring,
        half_out[0], half_out[1], squares, stream, gain_here,
        both_weights[0], both_weights[1], taps,
    )


def solution(mesh):
    in_specs = (
        P(("groups", "frame"), "head"),
        P(("groups", "frame"), "head"),
        P(("groups", "frame"), "head"),
        P(("groups", "frame"), "head"),
        P("head"),
        P("head", "frame"),
        P(),
        P("frame", "head"),
        P(None, "head"),
        P("head", "frame"),
    )
    out_specs = P(("groups", "frame"), "head")
    frames, heads = mesh.shape["frame"], mesh.shape["head"]

    def step(*args):
        group_tokens = args[0].shape[0] // mesh.shape["groups"]
        width, hidden = args[7].shape
        tokens_move = (
            group_tokens <= hidden
            and heads == 2
            and mesh.shape["groups"] == 2
            and group_tokens == frames * TPF
            and frames % 2 == 0
            and frames >= 4
            and hidden % (heads * frames) == 0
            and width % (heads * frames) == 0
            and args[5].shape[1] % (2 * frames) == 0
        )
        return jax.shard_map(
            token_body if tokens_move else body,
            mesh=mesh, in_specs=in_specs, out_specs=out_specs, check_vma=False,
        )(*args)

    return step
```

```python
import functools

import jax
import jax.numpy as jnp
from jax import lax
from jax.experimental import pallas as pl
from jax.experimental.pallas import tpu as pltpu
from jax.sharding import PartitionSpec as P

D = 2240
HEADS = 10
HEAD_DIM = 112
TPF = 128


def prefix(x, axis, combine, identity):
    length, place = (lax.axis_size(axis), lax.axis_index(axis))
    everything = jax.tree.map(lambda part: lax.all_gather(part, axis), x)
    start = jax.tree.map(
        lambda part, zero: jnp.broadcast_to(jnp.asarray(zero, part.dtype), part.shape), x, identity
    )

    def hop(k, before):
        reached = k < place
        new = combine(before, jax.tree.map(lambda part: part[k], everything))
        return jax.tree.map(lambda a, b: jnp.where(reached, a, b), new, before)

    return lax.fori_loop(0, length, hop, start)


def padded_2(block, sides, width):
    for axis, dim in sides:
        count = lax.axis_size(axis)
        forward = [(i, i + 1) for i in range(count - 1)]
        backward = [(target, source) for source, target in forward]
        low = lax.ppermute(
            lax.slice_in_dim(block, block.shape[dim] - width, None, axis=dim), axis, forward
        )
        high = lax.ppermute(lax.slice_in_dim(block, 0, width, axis=dim), axis, backward)
        block = jnp.concatenate([low, block, high], axis=dim)
    return block


def add_pair(earlier, later):
    return (earlier[0] + later[0], earlier[1] + later[1])


def body(
    stream, queries, key_rows, value_rows, attn_gain, w_out, ffn_gain, w_up, conv_taps, w_down
):
    highest = lax.Precision.HIGHEST
    tokens_here = queries.shape[0]
    frames_here = tokens_here // TPF
    heads_here = queries.shape[1] // HEAD_DIM
    qpos = jnp.maximum(queries.astype(jnp.float32), 0.0).reshape(
        frames_here, TPF, heads_here, HEAD_DIM
    )
    kpos = jnp.maximum(key_rows.astype(jnp.float32), 0.0).reshape(
        frames_here, TPF, heads_here, HEAD_DIM
    )
    values = value_rows.astype(jnp.float32).reshape(frames_here, TPF, heads_here, HEAD_DIM)
    frame_state = jnp.einsum("fthb,fthc->fhbc", kpos, values, precision=highest)
    frame_keys = jnp.sum(kpos, axis=1)
    own_state = jnp.sum(frame_state, axis=0)
    own_keys = jnp.sum(frame_keys, axis=0)
    empty_state = jnp.zeros_like(own_state)
    empty_keys = jnp.zeros_like(own_keys)
    before_state, before_keys = prefix(
        (own_state, own_keys), "frame", add_pair, (empty_state, empty_keys)
    )
    state = before_state[None] + jnp.cumsum(frame_state, axis=0)
    key_total = before_keys[None] + jnp.cumsum(frame_keys, axis=0)
    numer = jnp.einsum("fthb,fhbc->fthc", qpos, state, precision=highest)
    denom = jnp.einsum("fthb,fhb->fth", qpos, key_total, precision=highest) + 1e-06
    attended = (numer / denom[..., None]).reshape(tokens_here, heads_here * HEAD_DIM)
    squares = lax.psum(jnp.sum(attended * attended, axis=1), "head")
    scale = lax.rsqrt(squares / (HEADS * HEAD_DIM) + 1e-06)
    normed = (attended * scale[:, None] * attn_gain).astype(jnp.bfloat16)
    width_here = stream.shape[1]
    first_col = lax.axis_index("head") * width_here
    gain_here = lax.dynamic_slice_in_dim(ffn_gain, first_col, width_here, 0)
    proj = jnp.dot(
        normed,
        lax.all_gather(w_out, "frame", axis=1, tiled=True),
        preferred_element_type=jnp.float32,
    )
    proj_mine = lax.psum_scatter(proj, "head", scatter_dimension=1, tiled=True)
    resid_mine = (stream.astype(jnp.float32) + proj_mine).astype(jnp.bfloat16)
    resid_mine = lax.optimization_barrier(resid_mine)
    resid_float = resid_mine.astype(jnp.float32)
    total_sq = lax.psum(jnp.sum(resid_float * resid_float, axis=1), "head")
    inverse = lax.rsqrt(total_sq / D + 1e-06)
    normed_part = (resid_float * inverse[:, None] * gain_here).astype(jnp.bfloat16)
    ffn_in = lax.all_gather(normed_part, "head", axis=1, tiled=True)
    hidden_here = w_up.shape[1]
    up_value = jnp.dot(
        ffn_in,
        lax.all_gather(w_up, "frame", axis=0, tiled=True),
        preferred_element_type=jnp.float32,
    )
    hidden = (
        jax.nn.silu(up_value).astype(jnp.bfloat16).reshape(ffn_in.shape[0] // TPF, TPF, hidden_here)
    )
    padded = padded_2(hidden, (("frame", 0),), 1)
    padded_float = padded.astype(jnp.float32)
    mixed = (
        conv_taps[0] * padded_float[:-2]
        + conv_taps[1] * padded_float[1:-1]
        + conv_taps[2] * padded_float[2:]
    )
    mixed = mixed.astype(jnp.bfloat16).reshape(tokens_here, hidden_here)
    ffn_terms = jnp.dot(
        mixed,
        lax.all_gather(w_down, "frame", axis=1, tiled=True),
        preferred_element_type=jnp.float32,
    )
    ffn_mine = lax.psum_scatter(ffn_terms, "head", scatter_dimension=1, tiled=True)
    return (resid_float + ffn_mine).astype(jnp.bfloat16)


MESH_ID = pl.DeviceIdType.MESH


def ring_frame(pos, n):
    late = pos // (n // 2)
    return (1 - late) * (2 * pos) + late * (2 * (n - 1 - pos) + 1)


def ring_place(frame, n):
    odd = frame % 2
    return (1 - odd) * (frame // 2) + odd * (n - 1 - frame // 2)


def greet(partners):
    barrier = pltpu.get_barrier_semaphore()
    for partner in partners:
        pl.semaphore_signal(barrier, inc=1, device_id=partner, device_id_type=MESH_ID)
    pl.semaphore_wait(barrier, len(partners))


def remote(src, dst, send, recv, device):
    return pltpu.make_async_remote_copy(
        src_ref=src, dst_ref=dst, send_sem=send, recv_sem=recv,
        device_id=device, device_id_type=MESH_ID,
    )


def ring_steps(n):
    far = n // 2
    return [
        (step, way, half)
        for step in range(1, far + 1)
        for half in range(2)
        for way in range(2)
        if step < far or way == half
    ]


def ring_gather(buffer, place, n, send, recv, on_arrival, after_step):
    ends = [ring_frame((place + 1) % n, n), ring_frame((place + n - 1) % n, n)]
    started = []

    def origin(step, way):
        back = step if way == 0 else n - step
        return ring_frame((place + n - back) % n, n)

    def arrive(step, way, half):
        source = origin(step, way)
        slot = buffer(source, half)
        remote(slot, slot, send.at[way, step, half], recv.at[way, step, half],
               {"frame": ends[way]}).wait_recv()
        on_arrival(source, half)

    for step, way, half in ring_steps(n):
        if step > 1:
            arrive(step - 1, way, half)
        slot = buffer(origin(step - 1, way), half)
        copy = remote(slot, slot, send.at[way, step, half], recv.at[way, step, half],
                      {"frame": ends[way]})
        copy.start()
        started.append(copy)
        if way == 1 and half == 1:
            if step == n // 2:
                arrive(step - 1, 0, 1)
                arrive(step - 1, 1, 0)
            after_step([ring_frame(place, n)] if step == 1 else
                       [origin(step - 1, 0), origin(step - 1, 1)])
    for way in range(2):
        arrive(n // 2, way, way)
    after_step([origin(n // 2, 0)])
    return started


def first_kernel(n, state_ref, total_ref, query_ref, gain_ref, up_ref, down_ref, proj_ref,
                 weights, own_out, other_out, sq_out, states, merged, proj, blocks, here,
                 state_send, state_recv, proj_send, proj_recv, all_send, all_recv,
                 over_send, over_recv):
    frame, group = lax.axis_index("frame"), lax.axis_index("groups")
    place = ring_place(frame, n)
    over = {"groups": 1 - group}
    ends = [ring_frame((place + 1) % n, n), ring_frame((place + n - 1) % n, n)]
    far = n // 2
    part = weights.shape[3]
    local = [
        pltpu.make_async_copy(state_ref, states.at[frame], here.at[0]),
        pltpu.make_async_copy(proj_ref, proj.at[frame], here.at[1]),
    ]
    for copy in local:
        copy.start()
    for at, ref in enumerate((up_ref, down_ref)):
        for j in range(n):
            blocks[at, j] = ref[:, j * part:(j + 1) * part]
    for at in range(2):
        local.append(
            pltpu.make_async_copy(blocks.at[at, frame], weights.at[at, frame], here.at[2 + at])
        )
        local[-1].start()
    greet([{"frame": (frame + k) % n} for k in range(1, n)] + [over])
    local[0].wait()
    local[1].wait()

    def origin(step, way):
        back = step if way == 0 else n - step
        return ring_frame((place + n - back) % n, n)

    ring, pushed, swapped = [], [], []

    def state_copy(step, way, half, source):
        slot = states.at[source, half]
        return remote(slot, slot, state_send.at[way, step, half], state_recv.at[way, step, half],
                      {"frame": ends[way]})

    def proj_copy(step, way, source):
        slot = proj.at[source, group]
        return remote(slot, slot, proj_send.at[way, step], proj_recv.at[way, step],
                      {"frame": ends[way]})

    def swap(slot, at):
        copy = remote(slot, slot, over_send.at[at], over_recv.at[at], over)
        copy.start()
        swapped.append(copy)

    ways = list(range(1, n))
    ways.sort(key=lambda k: -min(k, n - k))
    for step in range(1, far + 1):
        for half in range(2):
            for way in range(2):
                if step == far and way != half:
                    continue
                if step > 1:
                    state_copy(step - 1, way, half, origin(step - 1, way)).wait_recv()
                copy = state_copy(step, way, half, origin(step - 1, way))
                copy.start()
                ring.append(copy)
        for way in range(2):
            if step > 1:
                source = origin(step - 1, way)
                proj_copy(step - 1, way, source).wait_recv()
            if step < far or way == 0:
                copy = proj_copy(step, way, origin(step - 1, way))
                copy.start()
                ring.append(copy)
            if step > 1:
                swap(proj.at[source, group], 2 * (step - 1) + way)
        for k in ways[2 * (step - 1):2 * step]:
            target = (frame + k) % n
            copy = remote(blocks.at[group, target], weights.at[group, frame], all_send.at[k],
                          all_recv.at[k], {"frame": target})
            copy.start()
            pushed.append(copy)
    for k in ways:
        source = (frame + n - k) % n
        slot = weights.at[group, source]
        remote(slot, slot, all_send.at[k], all_recv.at[k], {"frame": source}).wait_recv()
        swap(slot, 2 * far + k)
    proj_copy(far, 0, origin(far, 0)).wait_recv()
    swap(proj.at[origin(far, 0), group], 2 * far)
    for half in range(2):
        for way in range(2):
            last = far if way == half else far - 1
            state_copy(last, way, half, origin(last, way)).wait_recv()
    for copy in ring + pushed:
        copy.wait_send()

    def swapped_in(slot, at):
        remote(slot, slot, over_send.at[at], over_recv.at[at], over).wait_recv()

    for step in range(1, far):
        for way in range(2):
            swapped_in(proj.at[origin(step, way), 1 - group], 2 * step + way)
    swapped_in(proj.at[origin(far, 0), 1 - group], 2 * far)
    count = proj.shape[2]
    for at in range(n):
        for half in range(2):
            side, first_row = at // far, (2 * (at % far) + half) * count
            merged[side, first_row:first_row + count] = proj[at, half]
    heads_here = query_ref.shape[0]
    before = jnp.zeros(states.shape[1:], jnp.float32)
    for at in range(n):
        seen = jnp.where(at < frame, 1.0, 0.0)
        before = before + states[at].astype(jnp.float32) * seen
    before = before.reshape(-1, before.shape[-1])
    depth = query_ref.shape[1]
    squares, pieces = 0.0, []
    for at in range(heads_here):
        query = query_ref[at].astype(jnp.float32).T
        state = total_ref[at] + before[at * depth:(at + 1) * depth]
        both = jnp.dot(query, state, precision=lax.Precision.HIGHEST,
                       preferred_element_type=jnp.float32)
        attended = both[:, :depth] / (both[:, depth:depth + 1] + 1e-06)
        squares = squares + jnp.sum(attended * attended, axis=1, keepdims=True)
        pieces.append(attended)
    sq_out[...] = jnp.broadcast_to(squares, sq_out.shape)
    gained = (jnp.concatenate(pieces, axis=1) * gain_ref[...]).astype(jnp.bfloat16)
    head = lax.axis_index("head")
    own_out[...] = against(gained, merged[head])
    other_out[...] = against(gained, merged[1 - head])
    for k in ways:
        swapped_in(weights.at[1 - group, (frame + n - k) % n], 2 * far + k)
    for copy in swapped:
        copy.wait_send()
    local[2].wait()
    local[3].wait()


def second_kernel(n, features, width, own_ref, other_ref, sq_ref, stream_ref, gain_ref,
                  weights_ref, taps_ref, out_ref,
                  everything, resid, arrived, sq_in, sq_mine, sq_two, hidden, mixed, theirs,
                  twin_in, send_buf, recv_buf,
                  pair_send, pair_recv, ring_send, ring_recv, twin_send, twin_recv,
                  sum_twin_send, sum_twin_recv, sum_send, sum_recv):
    frame, head = lax.axis_index("frame"), lax.axis_index("head")
    place = ring_place(frame, n)
    twin = {"head": 1 - head}
    ends = [ring_frame((place + 1) % n, n), ring_frame((place + n - 1) % n, n)]
    far = n // 2
    rows = stream_ref.shape[0] // 2
    hidden[0] = jnp.zeros_like(hidden[0])
    hidden[n + 1] = jnp.zeros_like(hidden[0])
    greet([twin, {"frame": ends[0]}, {"frame": ends[1]}])
    first = remote(other_ref, arrived, pair_send.at[0], pair_recv.at[0], twin)
    second = remote(sq_ref, sq_in, pair_send.at[1], pair_recv.at[1], twin)
    second.start()
    first.start()
    second.wait()
    scale = lax.rsqrt((sq_ref[...] + sq_in[...])[:, :1] / features + 1e-06)
    first.wait()
    value = stream_ref[...].astype(jnp.float32) + (own_ref[...] + arrived[...]) * scale
    rounded = value.astype(jnp.bfloat16)
    resid[...] = rounded
    value = rounded.astype(jnp.float32)
    mine = jnp.broadcast_to(jnp.sum(value * value, axis=1, keepdims=True), sq_mine.shape)
    sq_mine[...] = mine
    third = remote(sq_mine, sq_two, pair_send.at[2], pair_recv.at[2], twin)
    third.start()
    third.wait()
    inverse = lax.rsqrt((mine + sq_two[...])[:, :1] / width + 1e-06)
    normed = (value * inverse * gain_ref[...]).astype(jnp.bfloat16)
    everything[head, frame, 0] = normed[:rows]
    everything[head, frame, 1] = normed[rows:]
    copies = []

    def to_twin(source, half):
        slot = everything.at[head, source, half]
        copy = remote(slot, slot, twin_send.at[source, half], twin_recv.at[source, half], twin)
        copy.start()
        copies.append(copy)

    def up_blocks(sources):
        for source in sources:
            for half in range(2):
                slot = everything.at[1 - head, source, half]
                remote(slot, slot, twin_send.at[source, half], twin_recv.at[source, half],
                       twin).wait_recv()
            total = None
            for at in range(2):
                block = jnp.concatenate(
                    [everything[at, source, 0], everything[at, source, 1]], axis=0
                )
                term = jnp.dot(block, weights_ref[0, at], preferred_element_type=jnp.float32)
                total = term if total is None else total + term
            act = total / (1.0 + jnp.exp(-total))
            hidden[source + 1] = act.astype(jnp.bfloat16).astype(jnp.float32)

    to_twin(frame, 0)
    to_twin(frame, 1)
    gathers = ring_gather(lambda source, half: everything.at[head, source, half], place, n,
                          ring_send, ring_recv, to_twin, up_blocks)

    def frame_of(way, ahead):
        return ring_frame((place + (ahead if way == 0 else n - ahead)) % n, n)

    twins = {}

    def produce(way, ahead):
        q = frame_of(way, ahead)
        blend = (
            taps_ref[0:1] * hidden[q] + taps_ref[1:2] * hidden[q + 1]
            + taps_ref[2:3] * hidden[q + 2]
        ).astype(jnp.bfloat16)
        mixed[q] = blend
        product = against(blend, weights_ref[1, 1 - head]).astype(jnp.bfloat16)
        for half in range(2):
            theirs[q, half] = product[half * rows:(half + 1) * rows]
            at = len(twins)
            copy = remote(theirs.at[q, half], twin_in.at[q, half], sum_twin_send.at[at],
                          sum_twin_recv.at[at], twin)
            copy.start()
            twins[way, ahead, half] = copy

    def produce_step(step):
        ahead = far + 1 - step
        produce(1, ahead)
        if 0 < ahead < far:
            produce(0, ahead)

    def terms(way, ahead):
        q = frame_of(way, ahead)
        own = against(mixed[q], weights_ref[1, head])
        out = []
        for half in range(2):
            twins[way, ahead, half].wait()
            out.append(own[half * rows:(half + 1) * rows]
                       + twin_in[q, half].astype(jnp.float32))
        return out

    def arrival(step, way, half):
        slot = recv_buf.at[way, step - 1, half]
        remote(slot, slot, sum_send.at[way, step, half], sum_recv.at[way, step, half],
               {"frame": ends[way]}).wait_recv()
        return recv_buf[way, step - 1, half].astype(jnp.float32)

    started = []

    def send_sum(step, way, half, total):
        if step > 2 or (step == 2 and way == half):
            total = total + arrival(step - 1, way, half)
        send_buf[way, step - 1, half] = total.astype(jnp.bfloat16)
        copy = remote(send_buf.at[way, step - 1, half], recv_buf.at[way, step - 1, half],
                      sum_send.at[way, step, half], sum_recv.at[way, step, half],
                      {"frame": ends[way]})
        copy.start()
        started.append(copy)

    produce_step(1)
    produce_step(2)
    for step in range(1, far + 1):
        ahead = far + 1 - step
        if step == 1:
            held = terms(1, ahead)
            send_sum(1, 0, 0, held[0])
            send_sum(1, 1, 1, held[1])
        else:
            held = [terms(0, ahead), terms(1, ahead)]
            for half in range(2):
                for way in range(2):
                    send_sum(step, way, half, held[way][half])
        if step < far:
            produce_step(step + 2)
    held = terms(1, 0)
    for half in range(2):
        total = held[half]
        for way in range(2):
            total = total + arrival(far, way, half)
        block = resid[half * rows:(half + 1) * rows].astype(jnp.float32)
        out_ref[half * rows:(half + 1) * rows] = (block + total).astype(jnp.bfloat16)
    for copy in started + copies + gathers:
        copy.wait_send()


def against(x, y):
    return lax.dot_general(x, y, (((1,), (1,)), ((), ())), preferred_element_type=jnp.float32)


VMEM = pl.BlockSpec(memory_space=pltpu.VMEM)


def call(kernel, ident, outs, scratch, *args):
    return pl.pallas_call(
        kernel,
        out_shape=outs,
        in_specs=[VMEM] * len(args),
        out_specs=[VMEM] * len(outs) if isinstance(outs, (list, tuple)) else VMEM,
        scratch_shapes=scratch,
        compiler_params=pltpu.CompilerParams(
            collective_id=ident, has_side_effects=True, vmem_limit_bytes=48 * 2**20
        ),
    )(*args)


def token_body(
    stream, queries, key_rows, value_rows, attn_gain, w_out, ffn_gain, w_up, conv_taps, w_down
):
    n = lax.axis_size("frame")
    frame, head = lax.axis_index("frame"), lax.axis_index("head")
    f32, bf16 = jnp.float32, jnp.bfloat16
    tokens = queries.shape[0]
    heads_here = queries.shape[1] // HEAD_DIM
    dma = pltpu.SemaphoreType.DMA
    far = n // 2
    ring = [dma((2, far + 1, 2)), dma((2, far + 1, 2))]

    def split(x):
        return x.reshape(tokens, heads_here, HEAD_DIM)

    pad = 128
    kpos = split(jnp.maximum(key_rows, 0))
    ones = jnp.zeros((tokens, heads_here, pad - HEAD_DIM), bf16).at[:, :, 0].set(1)
    values = jnp.concatenate([split(value_rows), ones], axis=2)
    own_state = jnp.einsum("thb,thc->hbc", kpos, values, preferred_element_type=f32)
    sent = own_state.astype(bf16).reshape(2, heads_here * HEAD_DIM // 2, pad)

    up_rows, hidden = w_up.shape
    part = hidden // n
    out_cols = w_down.shape[1]
    width = stream.shape[1]
    query_t = jnp.maximum(queries, 0).T.reshape(heads_here, HEAD_DIM, tokens)
    weights, half_own, half_other, squares = call(
        functools.partial(first_kernel, n), 0,
        [
            jax.ShapeDtypeStruct((2, n, up_rows, part), bf16),
            jax.ShapeDtypeStruct((tokens, width), f32),
            jax.ShapeDtypeStruct((tokens, width), f32),
            jax.ShapeDtypeStruct((tokens, 128), f32),
        ],
        [pltpu.VMEM((n,) + sent.shape, bf16),
         pltpu.VMEM((2, width, w_out.shape[0]), bf16),
         pltpu.VMEM((n, 2, out_cols // 2, w_out.shape[0]), bf16),
         pltpu.VMEM((2, n, up_rows, part), bf16), dma((4,))] + ring
        + [dma((2, far + 1)), dma((2, far + 1)), dma((n,)), dma((n,)), dma((2 * n,)), dma((2 * n,))],
        sent, own_state, query_t, attn_gain[None], w_up, w_down.T,
        w_out.T.reshape(2, out_cols // 2, w_out.shape[0]),
    )
    gain_here = lax.dynamic_slice_in_dim(ffn_gain, head * width, width, 0)[None]
    taps = lax.dynamic_slice_in_dim(conv_taps, frame * part, part, 1)
    both_weights = weights.reshape(2, 2, width, part)
    shape = (n, 2, tokens // 2, width)
    link = (2, far, 2, tokens // 2, width)
    return call(
        functools.partial(second_kernel, n, HEADS * HEAD_DIM, D), 1,
        jax.ShapeDtypeStruct((tokens, width), bf16),
        [
            pltpu.VMEM((2,) + shape, bf16),
            pltpu.VMEM((tokens, width), bf16),
            pltpu.VMEM((tokens, width), f32),
            pltpu.VMEM((tokens, 128), f32),
            pltpu.VMEM((tokens, 128), f32),
            pltpu.VMEM((tokens, 128), f32),
            pltpu.VMEM((n + 2, tokens, part), f32),
            pltpu.VMEM((n, tokens, part), bf16),
            pltpu.VMEM(shape, bf16),
            pltpu.VMEM(shape, bf16),
            pltpu.VMEM(link, bf16),
            pltpu.VMEM(link, bf16),
            dma((3,)), dma((3,)),
        ] + ring + [dma((n, 2)), dma((n, 2)), dma((2 * n,)), dma((2 * n,))] + ring,
        half_own, half_other, squares, stream, gain_here,
        both_weights, taps,
    )


def solution(mesh):
    in_specs = (
        P(("groups", "frame"), "head"),
        P(("groups", "frame"), "head"),
        P(("groups", "frame"), "head"),
        P(("groups", "frame"), "head"),
        P("head"),
        P("head", "frame"),
        P(),
        P("frame", "head"),
        P(None, "head"),
        P("head", "frame"),
    )
    out_specs = P(("groups", "frame"), "head")
    frames, heads = mesh.shape["frame"], mesh.shape["head"]

    def step(*args):
        group_tokens = args[0].shape[0] // mesh.shape["groups"]
        width, hidden = args[7].shape
        tokens_move = (
            group_tokens <= hidden
            and heads == 2
            and mesh.shape["groups"] == 2
            and group_tokens == frames * TPF
            and frames % 2 == 0
            and frames >= 4
            and hidden % (heads * frames) == 0
            and width % (heads * frames) == 0
            and args[5].shape[1] % (2 * frames) == 0
        )
        return jax.shard_map(
            token_body if tokens_move else body,
            mesh=mesh, in_specs=in_specs, out_specs=out_specs, check_vma=False,
        )(*args)

    return step
```

```python
import functools

import jax
import jax.numpy as jnp
from jax import lax
from jax.experimental import pallas as pl
from jax.experimental.pallas import tpu as pltpu
from jax.sharding import PartitionSpec as P

D = 2240
HEADS = 10
HEAD_DIM = 112
TPF = 128


def prefix(x, axis, combine, identity):
    length, place = (lax.axis_size(axis), lax.axis_index(axis))
    everything = jax.tree.map(lambda part: lax.all_gather(part, axis), x)
    start = jax.tree.map(
        lambda part, zero: jnp.broadcast_to(jnp.asarray(zero, part.dtype), part.shape), x, identity
    )

    def hop(k, before):
        reached = k < place
        new = combine(before, jax.tree.map(lambda part: part[k], everything))
        return jax.tree.map(lambda a, b: jnp.where(reached, a, b), new, before)

    return lax.fori_loop(0, length, hop, start)


def padded_2(block, sides, width):
    for axis, dim in sides:
        count = lax.axis_size(axis)
        forward = [(i, i + 1) for i in range(count - 1)]
        backward = [(target, source) for source, target in forward]
        low = lax.ppermute(
            lax.slice_in_dim(block, block.shape[dim] - width, None, axis=dim), axis, forward
        )
        high = lax.ppermute(lax.slice_in_dim(block, 0, width, axis=dim), axis, backward)
        block = jnp.concatenate([low, block, high], axis=dim)
    return block


def add_pair(earlier, later):
    return (earlier[0] + later[0], earlier[1] + later[1])


def body(
    stream, queries, key_rows, value_rows, attn_gain, w_out, ffn_gain, w_up, conv_taps, w_down
):
    highest = lax.Precision.HIGHEST
    tokens_here = queries.shape[0]
    frames_here = tokens_here // TPF
    heads_here = queries.shape[1] // HEAD_DIM
    qpos = jnp.maximum(queries.astype(jnp.float32), 0.0).reshape(
        frames_here, TPF, heads_here, HEAD_DIM
    )
    kpos = jnp.maximum(key_rows.astype(jnp.float32), 0.0).reshape(
        frames_here, TPF, heads_here, HEAD_DIM
    )
    values = value_rows.astype(jnp.float32).reshape(frames_here, TPF, heads_here, HEAD_DIM)
    frame_state = jnp.einsum("fthb,fthc->fhbc", kpos, values, precision=highest)
    frame_keys = jnp.sum(kpos, axis=1)
    own_state = jnp.sum(frame_state, axis=0)
    own_keys = jnp.sum(frame_keys, axis=0)
    empty_state = jnp.zeros_like(own_state)
    empty_keys = jnp.zeros_like(own_keys)
    before_state, before_keys = prefix(
        (own_state, own_keys), "frame", add_pair, (empty_state, empty_keys)
    )
    state = before_state[None] + jnp.cumsum(frame_state, axis=0)
    key_total = before_keys[None] + jnp.cumsum(frame_keys, axis=0)
    numer = jnp.einsum("fthb,fhbc->fthc", qpos, state, precision=highest)
    denom = jnp.einsum("fthb,fhb->fth", qpos, key_total, precision=highest) + 1e-06
    attended = (numer / denom[..., None]).reshape(tokens_here, heads_here * HEAD_DIM)
    squares = lax.psum(jnp.sum(attended * attended, axis=1), "head")
    scale = lax.rsqrt(squares / (HEADS * HEAD_DIM) + 1e-06)
    normed = (attended * scale[:, None] * attn_gain).astype(jnp.bfloat16)
    width_here = stream.shape[1]
    first_col = lax.axis_index("head") * width_here
    gain_here = lax.dynamic_slice_in_dim(ffn_gain, first_col, width_here, 0)
    proj = jnp.dot(
        normed,
        lax.all_gather(w_out, "frame", axis=1, tiled=True),
        preferred_element_type=jnp.float32,
    )
    proj_mine = lax.psum_scatter(proj, "head", scatter_dimension=1, tiled=True)
    resid_mine = (stream.astype(jnp.float32) + proj_mine).astype(jnp.bfloat16)
    resid_mine = lax.optimization_barrier(resid_mine)
    resid_float = resid_mine.astype(jnp.float32)
    total_sq = lax.psum(jnp.sum(resid_float * resid_float, axis=1), "head")
    inverse = lax.rsqrt(total_sq / D + 1e-06)
    normed_part = (resid_float * inverse[:, None] * gain_here).astype(jnp.bfloat16)
    ffn_in = lax.all_gather(normed_part, "head", axis=1, tiled=True)
    hidden_here = w_up.shape[1]
    up_value = jnp.dot(
        ffn_in,
        lax.all_gather(w_up, "frame", axis=0, tiled=True),
        preferred_element_type=jnp.float32,
    )
    hidden = (
        jax.nn.silu(up_value).astype(jnp.bfloat16).reshape(ffn_in.shape[0] // TPF, TPF, hidden_here)
    )
    padded = padded_2(hidden, (("frame", 0),), 1)
    padded_float = padded.astype(jnp.float32)
    mixed = (
        conv_taps[0] * padded_float[:-2]
        + conv_taps[1] * padded_float[1:-1]
        + conv_taps[2] * padded_float[2:]
    )
    mixed = mixed.astype(jnp.bfloat16).reshape(tokens_here, hidden_here)
    ffn_terms = jnp.dot(
        mixed,
        lax.all_gather(w_down, "frame", axis=1, tiled=True),
        preferred_element_type=jnp.float32,
    )
    ffn_mine = lax.psum_scatter(ffn_terms, "head", scatter_dimension=1, tiled=True)
    return (resid_float + ffn_mine).astype(jnp.bfloat16)


MESH_ID = pl.DeviceIdType.MESH


def ring_frame(pos, n):
    late = pos // (n // 2)
    return (1 - late) * (2 * pos) + late * (2 * (n - 1 - pos) + 1)


def ring_place(frame, n):
    odd = frame % 2
    return (1 - odd) * (frame // 2) + odd * (n - 1 - frame // 2)


def greet(partners):
    barrier = pltpu.get_barrier_semaphore()
    for partner in partners:
        pl.semaphore_signal(barrier, inc=1, device_id=partner, device_id_type=MESH_ID)
    pl.semaphore_wait(barrier, len(partners))


def remote(src, dst, send, recv, device):
    return pltpu.make_async_remote_copy(
        src_ref=src, dst_ref=dst, send_sem=send, recv_sem=recv,
        device_id=device, device_id_type=MESH_ID,
    )


def ring_steps(n):
    far = n // 2
    return [
        (step, way, half)
        for step in range(1, far + 1)
        for half in range(2)
        for way in range(2)
        if step < far or way == half
    ]


def ring_gather(buffer, place, n, send, recv, on_arrival, after_step):
    ends = [ring_frame((place + 1) % n, n), ring_frame((place + n - 1) % n, n)]
    started = []

    def origin(step, way):
        back = step if way == 0 else n - step
        return ring_frame((place + n - back) % n, n)

    def arrive(step, way, half):
        source = origin(step, way)
        slot = buffer(source, half)
        remote(slot, slot, send.at[way, step, half], recv.at[way, step, half],
               {"frame": ends[way]}).wait_recv()
        on_arrival(source, half)

    for step, way, half in ring_steps(n):
        if step > 1:
            arrive(step - 1, way, half)
        slot = buffer(origin(step - 1, way), half)
        copy = remote(slot, slot, send.at[way, step, half], recv.at[way, step, half],
                      {"frame": ends[way]})
        copy.start()
        started.append(copy)
        if way == 1 and half == 1:
            if step == n // 2:
                arrive(step - 1, 0, 1)
                arrive(step - 1, 1, 0)
            after_step([ring_frame(place, n)] if step == 1 else
                       [origin(step - 1, 0), origin(step - 1, 1)])
    for way in range(2):
        arrive(n // 2, way, way)
    after_step([origin(n // 2, 0)])
    return started


def first_kernel(n, state_ref, total_ref, query_ref, gain_ref, up_ref, down_ref, proj_ref,
                 weights, own_out, other_out, sq_out, states, merged, proj, blocks, here,
                 state_send, state_recv, proj_send, proj_recv, all_send, all_recv,
                 over_send, over_recv):
    frame, group = lax.axis_index("frame"), lax.axis_index("groups")
    place = ring_place(frame, n)
    over = {"groups": 1 - group}
    ends = [ring_frame((place + 1) % n, n), ring_frame((place + n - 1) % n, n)]
    far = n // 2
    part = weights.shape[3]
    local = [
        pltpu.make_async_copy(state_ref, states.at[frame], here.at[0]),
        pltpu.make_async_copy(proj_ref, proj.at[frame], here.at[1]),
    ]
    for copy in local:
        copy.start()
    for at, ref in enumerate((up_ref, down_ref)):
        for j in range(n):
            blocks[at, j] = ref[:, j * part:(j + 1) * part]
    for at in range(2):
        local.append(
            pltpu.make_async_copy(blocks.at[at, frame], weights.at[at, frame], here.at[2 + at])
        )
        local[-1].start()
    greet([{"frame": (frame + k) % n} for k in range(1, n)]
          + [over, {"head": 1 - lax.axis_index("head")}])
    local[0].wait()
    local[1].wait()

    def origin(step, way):
        back = step if way == 0 else n - step
        return ring_frame((place + n - back) % n, n)

    ring, pushed, swapped = [], [], []

    def state_copy(step, way, half, source):
        slot = states.at[source, half]
        return remote(slot, slot, state_send.at[way, step, half], state_recv.at[way, step, half],
                      {"frame": ends[way]})

    def proj_copy(step, way, source):
        slot = proj.at[source, group]
        return remote(slot, slot, proj_send.at[way, step], proj_recv.at[way, step],
                      {"frame": ends[way]})

    def swap(slot, at):
        copy = remote(slot, slot, over_send.at[at], over_recv.at[at], over)
        copy.start()
        swapped.append(copy)

    ways = list(range(1, n))
    ways.sort(key=lambda k: -min(k, n - k))
    for step in range(1, far + 1):
        for half in range(2):
            for way in range(2):
                if step == far and way != half:
                    continue
                if step > 1:
                    state_copy(step - 1, way, half, origin(step - 1, way)).wait_recv()
                copy = state_copy(step, way, half, origin(step - 1, way))
                copy.start()
                ring.append(copy)
        for way in range(2):
            if step > 1:
                source = origin(step - 1, way)
                proj_copy(step - 1, way, source).wait_recv()
            if step < far or way == 0:
                copy = proj_copy(step, way, origin(step - 1, way))
                copy.start()
                ring.append(copy)
            if step > 1:
                swap(proj.at[source, group], 2 * (step - 1) + way)
        for k in ways[2 * (step - 1):2 * step]:
            target = (frame + k) % n
            copy = remote(blocks.at[group, target], weights.at[group, frame], all_send.at[k],
                          all_recv.at[k], {"frame": target})
            copy.start()
            pushed.append(copy)
    for k in ways:
        source = (frame + n - k) % n
        slot = weights.at[group, source]
        remote(slot, slot, all_send.at[k], all_recv.at[k], {"frame": source}).wait_recv()
        swap(slot, 2 * far + k)
    proj_copy(far, 0, origin(far, 0)).wait_recv()
    swap(proj.at[origin(far, 0), group], 2 * far)
    for half in range(2):
        for way in range(2):
            last = far if way == half else far - 1
            state_copy(last, way, half, origin(last, way)).wait_recv()
    def swapped_in(slot, at):
        remote(slot, slot, over_send.at[at], over_recv.at[at], over).wait_recv()

    for step in range(1, far):
        for way in range(2):
            swapped_in(proj.at[origin(step, way), 1 - group], 2 * step + way)
    swapped_in(proj.at[origin(far, 0), 1 - group], 2 * far)
    count = proj.shape[2]
    for at in range(n):
        for half in range(2):
            side, first_row = at // far, (2 * (at % far) + half) * count
            merged[side, first_row:first_row + count] = proj[at, half]
    heads_here = query_ref.shape[0]
    before = jnp.zeros(states.shape[1:], jnp.float32)
    for at in range(n):
        seen = jnp.where(at < frame, 1.0, 0.0)
        before = before + states[at].astype(jnp.float32) * seen
    before = before.reshape(-1, before.shape[-1])
    depth = query_ref.shape[1]
    squares, pieces = 0.0, []
    for at in range(heads_here):
        query = query_ref[at].astype(jnp.float32).T
        state = total_ref[at] + before[at * depth:(at + 1) * depth]
        both = jnp.dot(query, state, precision=lax.Precision.HIGHEST,
                       preferred_element_type=jnp.float32)
        attended = both[:, :depth] / (both[:, depth:depth + 1] + 1e-06)
        squares = squares + jnp.sum(attended * attended, axis=1, keepdims=True)
        pieces.append(attended)
    sq_out[...] = jnp.broadcast_to(squares, sq_out.shape)
    gained = (jnp.concatenate(pieces, axis=1) * gain_ref[...]).astype(jnp.bfloat16)
    head = lax.axis_index("head")
    own_out[...] = against(gained, merged[head])
    other_out[...] = against(gained, merged[1 - head])

    def ready():
        for k in ways:
            swapped_in(weights.at[1 - group, (frame + n - k) % n], 2 * far + k)
        local[2].wait()
        local[3].wait()

    return ready, ring + pushed + swapped


def second_kernel(n, features, width, ready, own_ref, other_ref, sq_ref, stream_ref, gain_ref,
                  weights_ref, taps_ref, out_ref,
                  everything, resid, arrived, sq_in, sq_mine, sq_two, hidden, mixed, theirs,
                  twin_in, send_buf, recv_buf,
                  pair_send, pair_recv, ring_send, ring_recv, twin_send, twin_recv,
                  sum_twin_send, sum_twin_recv, sum_send, sum_recv):
    frame, head = lax.axis_index("frame"), lax.axis_index("head")
    place = ring_place(frame, n)
    twin = {"head": 1 - head}
    ends = [ring_frame((place + 1) % n, n), ring_frame((place + n - 1) % n, n)]
    far = n // 2
    rows = stream_ref.shape[0] // 2
    hidden[0] = jnp.zeros_like(hidden[0])
    hidden[n + 1] = jnp.zeros_like(hidden[0])
    first = remote(other_ref, arrived, pair_send.at[0], pair_recv.at[0], twin)
    second = remote(sq_ref, sq_in, pair_send.at[1], pair_recv.at[1], twin)
    second.start()
    first.start()
    second.wait()
    scale = lax.rsqrt((sq_ref[...] + sq_in[...])[:, :1] / features + 1e-06)
    first.wait()
    value = stream_ref[...].astype(jnp.float32) + (own_ref[...] + arrived[...]) * scale
    rounded = value.astype(jnp.bfloat16)
    resid[...] = rounded
    value = rounded.astype(jnp.float32)
    mine = jnp.broadcast_to(jnp.sum(value * value, axis=1, keepdims=True), sq_mine.shape)
    sq_mine[...] = mine
    third = remote(sq_mine, sq_two, pair_send.at[2], pair_recv.at[2], twin)
    third.start()
    third.wait()
    inverse = lax.rsqrt((mine + sq_two[...])[:, :1] / width + 1e-06)
    normed = (value * inverse * gain_ref[...]).astype(jnp.bfloat16)
    everything[head, frame, 0] = normed[:rows]
    everything[head, frame, 1] = normed[rows:]
    copies = []

    def to_twin(source, half):
        slot = everything.at[head, source, half]
        copy = remote(slot, slot, twin_send.at[source, half], twin_recv.at[source, half], twin)
        copy.start()
        copies.append(copy)

    waiting = []

    def weights_of(which, side):
        return jnp.concatenate(
            [weights_ref[which, side * far + at] for at in range(far)], axis=0
        )

    def up_blocks(sources):
        waiting.extend(sources)
        if len(waiting) < n - 1:
            return
        if len(waiting) == n - 1:
            ready()
        for source in waiting if len(waiting) == n - 1 else sources:
            for half in range(2):
                slot = everything.at[1 - head, source, half]
                remote(slot, slot, twin_send.at[source, half], twin_recv.at[source, half],
                       twin).wait_recv()
            total = None
            for at in range(2):
                block = jnp.concatenate(
                    [everything[at, source, 0], everything[at, source, 1]], axis=0
                )
                term = jnp.dot(block, weights_of(0, at), preferred_element_type=jnp.float32)
                total = term if total is None else total + term
            act = total / (1.0 + jnp.exp(-total))
            hidden[source + 1] = act.astype(jnp.bfloat16).astype(jnp.float32)

    to_twin(frame, 0)
    to_twin(frame, 1)
    gathers = ring_gather(lambda source, half: everything.at[head, source, half], place, n,
                          ring_send, ring_recv, to_twin, up_blocks)

    def frame_of(way, ahead):
        return ring_frame((place + (ahead if way == 0 else n - ahead)) % n, n)

    twins = {}

    def produce(way, ahead):
        q = frame_of(way, ahead)
        blend = (
            taps_ref[0:1] * hidden[q] + taps_ref[1:2] * hidden[q + 1]
            + taps_ref[2:3] * hidden[q + 2]
        ).astype(jnp.bfloat16)
        mixed[q] = blend
        product = against(blend, weights_of(1, 1 - head)).astype(jnp.bfloat16)
        for half in range(2):
            theirs[q, half] = product[half * rows:(half + 1) * rows]
            at = len(twins)
            copy = remote(theirs.at[q, half], twin_in.at[q, half], sum_twin_send.at[at],
                          sum_twin_recv.at[at], twin)
            copy.start()
            twins[way, ahead, half] = copy

    def produce_step(step):
        ahead = far + 1 - step
        produce(1, ahead)
        if 0 < ahead < far:
            produce(0, ahead)

    def terms(way, ahead):
        q = frame_of(way, ahead)
        own = against(mixed[q], weights_of(1, head))
        out = []
        for half in range(2):
            twins[way, ahead, half].wait()
            out.append(own[half * rows:(half + 1) * rows]
                       + twin_in[q, half].astype(jnp.float32))
        return out

    def arrival(step, way, half):
        slot = recv_buf.at[way, step - 1, half]
        remote(slot, slot, sum_send.at[way, step, half], sum_recv.at[way, step, half],
               {"frame": ends[way]}).wait_recv()
        return recv_buf[way, step - 1, half].astype(jnp.float32)

    started = []

    def send_sum(step, way, half, total):
        if step > 2 or (step == 2 and way == half):
            total = total + arrival(step - 1, way, half)
        send_buf[way, step - 1, half] = total.astype(jnp.bfloat16)
        copy = remote(send_buf.at[way, step - 1, half], recv_buf.at[way, step - 1, half],
                      sum_send.at[way, step, half], sum_recv.at[way, step, half],
                      {"frame": ends[way]})
        copy.start()
        started.append(copy)

    produce_step(1)
    produce_step(2)
    for step in range(1, far + 1):
        ahead = far + 1 - step
        if step == 1:
            held = terms(1, ahead)
            send_sum(1, 0, 0, held[0])
            send_sum(1, 1, 1, held[1])
        else:
            held = [terms(0, ahead), terms(1, ahead)]
            for half in range(2):
                for way in range(2):
                    send_sum(step, way, half, held[way][half])
        if step < far:
            produce_step(step + 2)
    held = terms(1, 0)
    for half in range(2):
        total = held[half]
        for way in range(2):
            total = total + arrival(far, way, half)
        block = resid[half * rows:(half + 1) * rows].astype(jnp.float32)
        out_ref[half * rows:(half + 1) * rows] = (block + total).astype(jnp.bfloat16)
    for copy in started + copies + gathers:
        copy.wait_send()


def against(x, y):
    return lax.dot_general(x, y, (((1,), (1,)), ((), ())), preferred_element_type=jnp.float32)


def whole_kernel(n, features, width, state_ref, total_ref, query_ref, gain_ref, up_ref, down_ref,
                 proj_ref, stream_ref, ffn_gain_ref, taps_ref, out_ref,
                 weights, own, other, squares, *scratch):
    ready, sent = first_kernel(
        n, state_ref, total_ref, query_ref, gain_ref, up_ref, down_ref, proj_ref,
        weights, own, other, squares, *scratch[:13],
    )
    second_kernel(
        n, features, width, ready, own, other, squares, stream_ref, ffn_gain_ref,
        weights, taps_ref, out_ref, *scratch[13:],
    )
    for copy in sent:
        copy.wait_send()


VMEM = pl.BlockSpec(memory_space=pltpu.VMEM)


def call(kernel, ident, outs, scratch, *args):
    return pl.pallas_call(
        kernel,
        out_shape=outs,
        in_specs=[VMEM] * len(args),
        out_specs=[VMEM] * len(outs) if isinstance(outs, (list, tuple)) else VMEM,
        scratch_shapes=scratch,
        compiler_params=pltpu.CompilerParams(
            collective_id=ident, has_side_effects=True, vmem_limit_bytes=48 * 2**20
        ),
    )(*args)


def token_body(
    stream, queries, key_rows, value_rows, attn_gain, w_out, ffn_gain, w_up, conv_taps, w_down
):
    n = lax.axis_size("frame")
    frame, head = lax.axis_index("frame"), lax.axis_index("head")
    f32, bf16 = jnp.float32, jnp.bfloat16
    tokens = queries.shape[0]
    heads_here = queries.shape[1] // HEAD_DIM
    dma = pltpu.SemaphoreType.DMA
    far = n // 2
    ring = [dma((2, far + 1, 2)), dma((2, far + 1, 2))]

    def split(x):
        return x.reshape(tokens, heads_here, HEAD_DIM)

    pad = 128
    kpos = split(jnp.maximum(key_rows, 0))
    ones = jnp.zeros((tokens, heads_here, pad - HEAD_DIM), bf16).at[:, :, 0].set(1)
    values = jnp.concatenate([split(value_rows), ones], axis=2)
    own_state = jnp.einsum("thb,thc->hbc", kpos, values, preferred_element_type=f32)
    sent = own_state.astype(bf16).reshape(2, heads_here * HEAD_DIM // 2, pad)

    up_rows, hidden = w_up.shape
    part = hidden // n
    out_cols = w_down.shape[1]
    width = stream.shape[1]
    query_t = jnp.maximum(queries, 0).T.reshape(heads_here, HEAD_DIM, tokens)
    gain_here = lax.dynamic_slice_in_dim(ffn_gain, head * width, width, 0)[None]
    taps = lax.dynamic_slice_in_dim(conv_taps, frame * part, part, 1)
    shape = (n, 2, tokens // 2, width)
    link = (2, far, 2, tokens // 2, width)
    return call(
        functools.partial(whole_kernel, n, HEADS * HEAD_DIM, D), 0,
        jax.ShapeDtypeStruct((tokens, width), bf16),
        [
            pltpu.VMEM((2, n, up_rows, part), bf16),
            pltpu.VMEM((tokens, width), f32),
            pltpu.VMEM((tokens, width), f32),
            pltpu.VMEM((tokens, 128), f32),
            pltpu.VMEM((n,) + sent.shape, bf16),
            pltpu.VMEM((2, width, w_out.shape[0]), bf16),
            pltpu.VMEM((n, 2, out_cols // 2, w_out.shape[0]), bf16),
            pltpu.VMEM((2, n, up_rows, part), bf16),
            dma((4,)),
        ] + ring + [
            dma((2, far + 1)), dma((2, far + 1)), dma((n,)), dma((n,)), dma((2 * n,)), dma((2 * n,)),
            pltpu.VMEM((2,) + shape, bf16),
            pltpu.VMEM((tokens, width), bf16),
            pltpu.VMEM((tokens, width), f32),
            pltpu.VMEM((tokens, 128), f32),
            pltpu.VMEM((tokens, 128), f32),
            pltpu.VMEM((tokens, 128), f32),
            pltpu.VMEM((n + 2, tokens, part), f32),
            pltpu.VMEM((n, tokens, part), bf16),
            pltpu.VMEM(shape, bf16),
            pltpu.VMEM(shape, bf16),
            pltpu.VMEM(link, bf16),
            pltpu.VMEM(link, bf16),
            dma((3,)), dma((3,)),
        ] + ring + [dma((n, 2)), dma((n, 2)), dma((2 * n,)), dma((2 * n,))] + ring,
        sent, own_state, query_t, attn_gain[None], w_up, w_down.T,
        w_out.T.reshape(2, out_cols // 2, w_out.shape[0]), stream, gain_here, taps,
    )


def solution(mesh):
    in_specs = (
        P(("groups", "frame"), "head"),
        P(("groups", "frame"), "head"),
        P(("groups", "frame"), "head"),
        P(("groups", "frame"), "head"),
        P("head"),
        P("head", "frame"),
        P(),
        P("frame", "head"),
        P(None, "head"),
        P("head", "frame"),
    )
    out_specs = P(("groups", "frame"), "head")
    frames, heads = mesh.shape["frame"], mesh.shape["head"]

    def step(*args):
        group_tokens = args[0].shape[0] // mesh.shape["groups"]
        width, hidden = args[7].shape
        tokens_move = (
            group_tokens <= hidden
            and heads == 2
            and mesh.shape["groups"] == 2
            and group_tokens == frames * TPF
            and frames % 2 == 0
            and frames >= 4
            and hidden % (heads * frames) == 0
            and width % (heads * frames) == 0
            and args[5].shape[1] % (2 * frames) == 0
        )
        return jax.shard_map(
            token_body if tokens_move else body,
            mesh=mesh, in_specs=in_specs, out_specs=out_specs, check_vma=False,
        )(*args)

    return step
```
